32 devices in a mesh: cuts: 4 (over z), rcv: 8 (over y, x, core).
Axes of the slice: x: 2, y: 2, z: 4, core: 2. Of those that a mesh axis runs over, the one named last changes fastest.
Arguments:
- down_spectra: float32 [8, 2048, 2560], P('cuts', 'rcv'), parts along dimension 0, may hold values from -0.07905694 to 0.07905694, as said below
- up_sources: float32 [8, 128, 2560], P('cuts', 'rcv'), parts along dimension 0, may hold values from -6 to 6
Outputs:
- solution: float32 [8, 2048, 128], P('cuts', 'rcv'), parts along dimension 0
- residual: float32 [8, 2048, 128], P('cuts', 'rcv'), parts along dimension 0
The draws below stay inside these ranges and needn't reach their ends.
There are 4 independent parts, one for each index of `cuts`. The reference program is written for one: setup_inputs(seed, part) draws one part's arguments, and reference() takes and returns one part's arrays. A program takes and returns all parts, laid end to end along the dimension named above; each array names one. Nothing has to cross between parts.
Inputs may be any that keep to these rules, and one draw needn't show every extreme that they name: `down_spectra`: real-valued entries.
All inputs are finite; a program needn't handle non-finite values.
Results may differ from the reference program's by a relative error of at most 0.00021.
Values sent between devices are 32-bit elements; how exact they have to be, the bound alone decides.
No kernel may reach another device: no remote copies, remote signals or barrier semaphores. Data moves between devices by JAX's collectives and lax.ppermute only.
A program may use at most 64 MiB of HBM per device.

```python
import math
import jax
import jax.numpy as jnp
from jax import lax

R = 2048
S = 2560
NV = 128
ITERS = 2


def draw_down_spectra(key, part):
    keys = jax.random.split(key, 3)
    position = jnp.arange(R, dtype=jnp.float32) / (R - 1)
    rising = jnp.exp(math.log(3.0) * (position - 0.5))
    spread = math.log(2.0)
    values = jnp.clip(jax.random.normal(keys[2], (2, R, S), jnp.float32), -6.0, 6.0)
    row_scale = rising * jnp.exp(jax.random.uniform(keys[0], (R,), jnp.float32, -spread, spread))
    shot_scale = jnp.exp(jax.random.uniform(keys[1], (S,), jnp.float32, -spread, spread))
    limit = 4.0 / math.sqrt(S)
    result = values * row_scale[None, :, None] * shot_scale[None, None, :] / math.sqrt(S)
    return jnp.clip(result, -limit, limit)


def block_levels(rng, dims, shards, least, top_value):
    factor_of = 1.0
    for axis_at, shards_of in shards:
        steps = jax.random.uniform(jax.random.fold_in(jax.random.fold_in(rng, 6), axis_at), (shards_of,), jnp.float32, least / len(shards), top_value / len(shards))
        factor_of = factor_of * jnp.repeat(jnp.exp(steps), dims[axis_at] // shards_of).reshape((-1,) + (1,) * (len(dims) - 1 - axis_at))
    return factor_of


def normal_values(key, dims, scale, most, shards=(), held_as=jnp.bfloat16):
    loudness = block_levels(key, dims, shards, -0.22, 0.18) if shards else 1.0
    array = jax.random.normal(key, dims, jnp.float32) * scale * loudness
    return jnp.minimum(jnp.maximum(array, -most), most).astype(held_as)


def setup_inputs(seed: int = 0, part: int = 0) -> dict:
    key_list = jax.random.split(jax.random.key(seed), 3)
    part_splits = jax.random.split(jax.random.fold_in(key_list[2], part), 3)
    down_spectra = draw_down_spectra(jax.random.fold_in(jax.random.fold_in(key_list[2], part), 71), part)
    up_sources = normal_values(part_splits[1], (2, NV, S), 1.0, 6.0, ((1, 8),), jnp.float32)
    return dict(down_spectra=down_spectra, up_sources=up_sources)


damping_ratio = 0.1


def product(left, right):
    return jnp.dot(left, right, precision=lax.Precision.HIGHEST, preferred_element_type=jnp.float32)


def product_left_t(left, right):
    return lax.dot_general(left, right, (((0,), (0,)), ((), ())), precision=lax.Precision.HIGHEST, preferred_element_type=jnp.float32)


def product_right_t(left, right):
    return lax.dot_general(left, right, (((1,), (1,)), ((), ())), precision=lax.Precision.HIGHEST, preferred_element_type=jnp.float32)


def complex_product(left, right):
    real_part = product(left[0], right[0]) - product(left[1], right[1])
    imag_part = product(left[0], right[1]) + product(left[1], right[0])
    return jnp.stack([real_part, imag_part])


def times_adjoint(left, right):
    real_part = product_right_t(left[0], right[0]) + product_right_t(left[1], right[1])
    imag_part = product_right_t(left[1], right[0]) - product_right_t(left[0], right[1])
    return jnp.stack([real_part, imag_part])


def adjoint_times(left, right):
    real_part = product_left_t(left[0], right[0]) + product_left_t(left[1], right[1])
    imag_part = product_left_t(left[0], right[1]) - product_left_t(left[1], right[0])
    return jnp.stack([real_part, imag_part])


def column_sum(first, second):
    return jnp.sum(first * second, axis=(0, 1))


def reference(down_spectra, up_sources):
    energy = jnp.sum(down_spectra * down_spectra)
    damping = damping_ratio * energy / R

    def operate(field):
        return complex_product(down_spectra, adjoint_times(down_spectra, field)) + damping * field

    rhs = times_adjoint(down_spectra, up_sources)
    solution = jnp.zeros_like(rhs)
    residual = rhs
    direction = rhs
    norm_now = column_sum(residual, residual)
    for iteration in range(ITERS):
        image = operate(direction)
        alpha = norm_now / column_sum(direction, image)
        solution = solution + alpha * direction
        residual = residual - alpha * image
        norm_next = column_sum(residual, residual)
        direction = residual + (norm_next / norm_now) * direction
        norm_now = norm_next
    return solution, residual
```

```python
import jax
import jax.numpy as jnp
from jax import lax
from jax.experimental import pallas as pl
from jax.experimental.pallas import tpu as pltpu
from jax.sharding import PartitionSpec as P

damping_ratio = 0.1
LANES = 128
f32 = jnp.float32
bf16 = jnp.bfloat16


def dot(left, right, right_dim):
    return lax.dot_general(left, right, (((1,), (right_dim,)), ((), ())), preferred_element_type=f32)


def parts_of(value):
    high = value.astype(bf16)
    return high, (value - high.astype(f32)).astype(bf16)


def call(kernel, outs, args, scratch=()):
    spec = pl.BlockSpec(memory_space=pltpu.VMEM)
    return pl.pallas_call(
        kernel,
        out_shape=[jax.ShapeDtypeStruct(shape, dtype) for shape, dtype in outs],
        in_specs=[spec] * len(args),
        out_specs=[spec] * len(outs),
        scratch_shapes=[pltpu.VMEM(shape, dtype) for shape, dtype in scratch],
        compiler_params=pltpu.CompilerParams(vmem_limit_bytes=40 << 20),
    )(*args)


def split_kernel(down_ref, high_ref, low_ref, energy_ref):
    rows, shots = down_ref.shape[1:]
    energy_ref[...] = jnp.zeros_like(energy_ref)

    def step(index, carry):
        at = pl.ds(pl.multiple_of(index * 16, 16), 16)
        for part in range(2):
            value = down_ref[part, at, :]
            high, low = parts_of(value)
            high_ref[part, at, :] = high
            low_ref[part, at, :] = low
            square = value * value
            energy_ref[...] += square[:8] + square[8:]
        return carry

    lax.fori_loop(0, rows // 16, step, 0)


def stage(value_ref, first_ref, second_ref, sign):
    half = value_ref.shape[0] // 2
    real = value_ref[:half, :]
    imag = value_ref[half:, :]
    for at, (a, b) in enumerate(zip(parts_of(real), parts_of(imag))):
        base = 2 * half * at
        first_ref[base : base + half, :] = a
        first_ref[base + half : base + 2 * half, :] = b
        second_ref[base : base + half, :] = b if sign > 0 else -b
        second_ref[base + half : base + 2 * half, :] = a if sign < 0 else -a


def apply_down(first, second, high_ref, low_ref, columns):
    count = first.shape[0] // 2
    total = dot(first, high_ref[0, :, columns], 1) + dot(second, high_ref[1, :, columns], 1)
    low = dot(first[:count], low_ref[0, :, columns], 1) + dot(second[:count], low_ref[1, :, columns], 1)
    return total[:count] + total[count:] + low


def apply_adjoint(first, second, high_ref, low_ref, columns):
    count = first.shape[0] // 2
    total = dot(first, high_ref[0, :, columns], 0) + dot(second, high_ref[1, :, columns], 0)
    low = dot(first[:count], low_ref[0, :, columns], 0) + dot(second[:count], low_ref[1, :, columns], 0)
    return total[:count] + total[count:] + low


def project(value_ref, first_ref, second_ref, blocks, columns):
    stage(value_ref, first_ref, second_ref, 1)
    rows = blocks[0][0].shape[1]
    total = 0.0
    for at, (high, low) in enumerate(blocks):
        own = slice(at * rows, (at + 1) * rows)
        total = total + apply_adjoint(first_ref[:, own], second_ref[:, own], high, low, columns)
    return total


def row_squares(value):
    return jnp.sum(value * value, axis=1, keepdims=True)


def both(value):
    half = value.shape[0] // 2
    total = value[:half] + value[half:]
    return jnp.concatenate([total, total], axis=0)


def tail(*columns):
    lane = lax.broadcasted_iota(jnp.int32, (columns[0].shape[0], LANES), 1)
    out = jnp.zeros(lane.shape, f32)
    for at, column in enumerate(columns):
        out = jnp.where(lane == at, column, out)
    return out


def rhs_kernel(sources, *refs):
    (real_ref, imag_ref, ha, la, ea, hb, lb, eb, rhs_ref, out_ref, x_ref, first_ref, second_ref, third_ref, fourth_ref) = refs
    half, shots = real_ref.shape
    x_ref[:half, :] = real_ref[...]
    x_ref[half:, :] = -imag_ref[...]
    stage(x_ref, first_ref, second_ref, -1)
    rows = ha.shape[1]
    every = slice(0, shots)
    for at, (high, low) in enumerate(((ha, la), (hb, lb))):
        rhs_ref[:, at * rows : (at + 1) * rows] = apply_down(first_ref[...], second_ref[...], high, low, every)
    front = out_ref.shape[1] - LANES
    out_ref[:, :front] = project(rhs_ref, third_ref, fourth_ref, ((ha, la), (hb, lb)), slice(0, front))
    energy = jnp.sum(ea[...] + eb[...])
    out_ref[:, front:] = tail(row_squares(rhs_ref[...]), jnp.full((2 * half, 1), energy, f32))


def back_kernel(*refs):
    (value_ref, ha, la, hb, lb, out_ref, first_ref, second_ref) = refs
    shots = ha.shape[2]
    out_ref[...] = project(value_ref, first_ref, second_ref, ((ha, la), (hb, lb)), slice(shots - out_ref.shape[1], shots))


def image_of(x_ref, first_ref, second_ref, blocks, image_ref, columns):
    stage(x_ref, first_ref, second_ref, -1)
    rows = blocks[0][0].shape[1]
    for at, (high, low) in enumerate(blocks):
        image_ref[:, at * rows : (at + 1) * rows] = apply_down(first_ref[...], second_ref[...], high, low, columns)


def first_kernel(receivers, *refs):
    (p0, p1, q0, q1, rhs_ref, ha, la, hb, lb) = refs[:9]
    (x_ref, scalar_ref, image_ref, residual_ref, out_ref, first_ref, second_ref, third_ref, fourth_ref) = refs[9:]
    front = p0.shape[1] - LANES
    x_ref[:, :front] = p0[:, :front] + p1[:, :front]
    x_ref[:, front:] = q0[...] + q1[...]
    ends = p0[:, front:] + p1[:, front:]
    norm = both(ends[:, 0:1])
    damping = damping_ratio * ends[:, 1:2] / receivers
    blocks = ((ha, la), (hb, lb))
    image_of(x_ref, first_ref, second_ref, blocks, image_ref, slice(0, x_ref.shape[1]))
    image = image_ref[...] + damping * rhs_ref[...]
    image_ref[...] = image
    alpha = norm / (both(row_squares(x_ref[...])) + damping * norm)
    residual = rhs_ref[...] - alpha * image
    residual_ref[...] = residual
    scalar_ref[...] = tail(norm, damping, alpha)
    out_ref[:, :front] = project(residual_ref, third_ref, fourth_ref, blocks, slice(0, front))
    out_ref[:, front:] = tail(row_squares(residual))


def last_kernel(*refs):
    (p0, p1, q0, q1, rhs_ref, before_ref, scalar_ref, image_ref, residual_ref, ha, la, hb, lb) = refs[:13]
    (keep_ref, give_ref, x_ref, y_ref, first_ref, second_ref) = refs[13:]
    front = p0.shape[1] - LANES
    x_ref[:, :front] = p0[:, :front] + p1[:, :front]
    x_ref[:, front:] = q0[...] + q1[...]
    following = both(p0[:, front : front + 1] + p1[:, front : front + 1])
    norm = scalar_ref[:, 0:1]
    damping = scalar_ref[:, 1:2]
    alpha = scalar_ref[:, 2:3]
    beta = following / norm
    image_of(x_ref, first_ref, second_ref, ((ha, la), (hb, lb)), y_ref, slice(0, x_ref.shape[1]))
    residual = residual_ref[...]
    image = y_ref[...] + beta * image_ref[...] + damping * residual
    curvature = both(row_squares(x_ref[...] + beta * before_ref[...])) + damping * (following + beta * following)
    alpha_next = following / curvature
    rhs = rhs_ref[...]
    found = alpha * rhs + alpha_next * (residual + beta * rhs)
    left = residual - alpha_next * image
    rows = ha.shape[1]
    keep_ref[0] = found[:, :rows]
    keep_ref[1] = left[:, :rows]
    give_ref[0] = found[:, rows:]
    give_ref[1] = left[:, rows:]


def swap(value, bit, count):
    return lax.ppermute(value, "rcv", [(at, at ^ (1 << bit)) for at in range(count)])


def body(down_spectra, up_sources, *, count, receivers):
    me = lax.axis_index("rcv")
    bits = count.bit_length() - 1
    chip_bits = list(range(1, bits))
    rows, shots = down_spectra.shape[1:]
    own = up_sources.shape[1]
    other_down = swap(down_spectra, 0, count)

    def gather(block, order):
        block = block.reshape((1,) * len(chip_bits) + block.shape)
        for bit in order:
            axis = len(chip_bits) - bit
            other = swap(block, bit, count)
            upper = ((me >> bit) & 1) == 1
            block = jnp.concatenate([jnp.where(upper, other, block), jnp.where(upper, block, other)], axis=axis)
        return block.reshape((-1, shots))

    real = gather(up_sources[0], chip_bits)
    imag = gather(up_sources[1], chip_bits[::-1])
    ha, la, ea = split(down_spectra)
    hb, lb, eb = split(other_down)
    columns = real.shape[0]
    packed = 2 * columns
    front = shots // 2
    wide = [((2 * packed, shots), bf16)] * 2
    short = [((2 * packed, 2 * rows), bf16)] * 2
    rhs, p = call(
        lambda *refs: rhs_kernel(None, *refs),
        [((packed, 2 * rows), f32), ((packed, front + LANES), f32)],
        (real, imag, ha, la, ea, hb, lb, eb),
        [((packed, shots), f32)] + wide + short,
    )
    (q,) = call(back_kernel, [((packed, shots - front), f32)], (rhs, ha, la, hb, lb), short)

    def exchange(p, q):
        for step in range(len(chip_bits) - 1):
            p = p + swap(p, chip_bits[step], count)
            q = q + swap(q, chip_bits[-1 - step], count)
        return p, swap(p, chip_bits[-1], count), q, swap(q, chip_bits[0], count)

    before, scalars, image, residual, p = call(
        lambda *refs: first_kernel(receivers, *refs),
        [
            ((packed, shots), f32),
            ((packed, LANES), f32),
            ((packed, 2 * rows), f32),
            ((packed, 2 * rows), f32),
            ((packed, front + LANES), f32),
        ],
        (*exchange(p, q), rhs, ha, la, hb, lb),
        wide + short,
    )
    (q,) = call(back_kernel, [((packed, shots - front), f32)], (residual, ha, la, hb, lb), short)
    keep, give = call(
        last_kernel,
        [((2, packed, rows), f32)] * 2,
        (*exchange(p, q), rhs, before, scalars, image, residual, ha, la, hb, lb),
        [((packed, shots), f32), ((packed, 2 * rows), f32)] + wide,
    )
    other = swap(give, 0, count)
    upper = (me & 1) == 1
    chips = count // 2

    def order(first, second):
        pair = jnp.stack([first.reshape(2, 2, chips, own, rows), second.reshape(2, 2, chips, own, rows)], axis=3)
        return pair.reshape(2, 2, chips * 2 * own, rows).transpose(0, 1, 3, 2)

    both_cores = order(jnp.where(upper, other, keep), jnp.where(upper, keep, other))
    return both_cores[0], both_cores[1]


def split(value):
    _, rows, shots = value.shape
    return call(
        split_kernel,
        [(value.shape, bf16), (value.shape, bf16), ((8, shots), f32)],
        (value,),
    )


def solution(mesh):
    count = mesh.shape["rcv"]

    def run(down_spectra, up_sources):
        return body(down_spectra, up_sources, count=count, receivers=down_spectra.shape[1] * count)

    specs = (P("cuts", "rcv", None), P("cuts", "rcv", None))
    return jax.shard_map(run, mesh=mesh, in_specs=specs, out_specs=specs, check_vma=False)
```

```python
import functools
import jax
import jax.numpy as jnp
from jax import lax
from jax.experimental import pallas as pl
from jax.experimental.pallas import tpu as pltpu
from jax.sharding import PartitionSpec as P

damping_ratio = 0.1
LANES = 128
GROUPS = 2
f32 = jnp.float32
bf16 = jnp.bfloat16


def dot(left, right):
    return lax.dot_general(left, right, (((1,), (0,)), ((), ())), preferred_element_type=f32)


def parts_of(value):
    high = value.astype(bf16)
    return high, (value - high.astype(f32)).astype(bf16)


def call(kernel, outs, args, scratch=()):
    spec = pl.BlockSpec(memory_space=pltpu.VMEM)
    return pl.pallas_call(
        kernel,
        out_shape=[jax.ShapeDtypeStruct(shape, dtype) for shape, dtype in outs],
        in_specs=[spec] * len(args),
        out_specs=[spec] * len(outs),
        scratch_shapes=[pltpu.VMEM(shape, dtype) for shape, dtype in scratch],
        compiler_params=pltpu.CompilerParams(vmem_limit_bytes=16 << 20),
    )(*args)


def split_kernel(down_ref, high_ref, low_ref, turned_high_ref, turned_low_ref, energy_ref):
    rows, shots = down_ref.shape[1:]
    width = 2 * LANES
    energy_ref[...] = jnp.zeros_like(energy_ref)

    def step(index, carry):
        at = pl.ds(pl.multiple_of(index * width, width), width)
        for part in range(2):
            value = down_ref[part, :, at]
            high, low = parts_of(value)
            high_ref[part, :, at] = high
            low_ref[part, :, at] = low
            turned_high_ref[part, at, :] = high.T
            turned_low_ref[part, at, :] = low.T
            energy_ref[...] += jnp.sum((value * value).reshape(rows // 8, 8, width), axis=0)
        return carry

    lax.fori_loop(0, shots // width, step, 0)


def split(value):
    _, rows, shots = value.shape
    plain, turned = ((2, rows, shots), bf16), ((2, shots, rows), bf16)
    high, low, turned_high, turned_low, energy = call(
        split_kernel, [plain, plain, turned, turned, ((8, 2 * LANES), f32)], (value,)
    )
    return (high, low), (turned_high, turned_low), energy


def stage(value_ref, first_ref, second_ref, sign):
    half = value_ref.shape[0] // 2
    real = value_ref[:half, :]
    imag = value_ref[half:, :]
    for at, (a, b) in enumerate(zip(parts_of(real), parts_of(imag))):
        base = 2 * half * at
        first_ref[base : base + half, :] = a
        first_ref[base + half : base + 2 * half, :] = b
        second_ref[base : base + half, :] = b if sign > 0 else -b
        second_ref[base + half : base + 2 * half, :] = a if sign < 0 else -a


def times(first, second, high_ref, low_ref, columns=slice(None)):
    count = first.shape[0] // 2
    total = dot(first, high_ref[0, :, columns]) + dot(second, high_ref[1, :, columns])
    low = dot(first[:count], low_ref[0, :, columns]) + dot(second[:count], low_ref[1, :, columns])
    return total[:count] + total[count:] + low


def row_squares(value):
    return jnp.sum(value * value, axis=1, keepdims=True)


def both(value):
    half = value.shape[0] // 2
    total = value[:half] + value[half:]
    return jnp.concatenate([total, total], axis=0)


def tail(*columns):
    lane = lax.broadcasted_iota(jnp.int32, (columns[0].shape[0], LANES), 1)
    out = jnp.zeros(lane.shape, f32)
    for at, column in enumerate(columns):
        out = jnp.where(lane == at, column, out)
    return out


def apply_down(x_ref, first_ref, second_ref, turned, image_ref):
    stage(x_ref, first_ref, second_ref, -1)
    rows = turned[0][0].shape[2]
    for at, (high, low) in enumerate(turned):
        image_ref[:, at * rows : (at + 1) * rows] = times(first_ref[...], second_ref[...], high, low)


def device_bit(bit):
    return (lax.axis_index("rcv") >> bit) & 1


def project(value_ref, first_ref, second_ref, plain, extra, outs, bits):
    stage(value_ref, first_ref, second_ref, 1)
    rows = plain[0][0].shape[1]
    shots = plain[0][0].shape[2]
    half = value_ref.shape[0] // 2
    for at, bit in enumerate(bits):
        columns = slice(at * shots // 2, (at + 1) * shots // 2)
        total = 0.0
        for block, (high, low) in enumerate(plain):
            own = slice(block * rows, (block + 1) * rows)
            total = total + times(first_ref[:, own], second_ref[:, own], high, low, columns)
        pieces = [(slice(0, shots // 2), total)]
        if at == 0:
            pieces.append((slice(shots // 2, shots // 2 + LANES), extra))
        keep_ref, give_ref = outs[2 * at : 2 * at + 2]
        upper = device_bit(bit) == 1
        for place, piece in pieces:
            keep_ref[:, place] = jnp.where(upper, piece[half:], piece[:half])
            give_ref[:, place] = jnp.where(upper, piece[:half], piece[half:])


def collect(pieces, x_ref, ends_ref, bits):
    front = x_ref.shape[1] // 2
    for at, bit in enumerate(bits):
        upper = device_bit(bit)
        for which, piece in enumerate(pieces[2 * at : 2 * at + 2]):
            half = piece.shape[0]
            place = pl.ds(pl.multiple_of((upper ^ which) * half, half), half)
            x_ref[place, at * front : (at + 1) * front] = piece[:, :front]
            if at == 0:
                ends_ref[place, :] = piece[:, front:]


def rhs_kernel(bits, *refs):
    real_ref, imag_ref, *refs = refs
    down, refs = refs[:8], refs[8:]
    (ea, eb), (rhs_ref, *outs), (x_ref, f0, s0, f1, s1) = refs[:2], refs[2:7], refs[7:]
    half = real_ref.shape[0]
    x_ref[:half, :] = real_ref[...]
    x_ref[half:, :] = -imag_ref[...]
    apply_down(x_ref, f0, s0, ((down[4], down[5]), (down[6], down[7])), rhs_ref)
    energy = jnp.full((2 * half, 1), jnp.sum(ea[...] + eb[...]), f32)
    extra = tail(row_squares(rhs_ref[...]), energy)
    project(rhs_ref, f1, s1, ((down[0], down[1]), (down[2], down[3])), extra, outs, bits)


def first_kernel(bits, receivers, *refs):
    pieces, (rhs_ref, *refs) = refs[:4], refs[4:]
    down, refs = refs[:8], refs[8:]
    (x_ref, scalar_ref, image_ref, residual_ref, *outs), (ends_ref, f0, s0, f1, s1) = refs[:8], refs[8:]
    collect(pieces, x_ref, ends_ref, bits)
    norm = both(ends_ref[:, 0:1])
    damping = damping_ratio * ends_ref[:, 1:2] / receivers
    apply_down(x_ref, f0, s0, ((down[4], down[5]), (down[6], down[7])), image_ref)
    image = image_ref[...] + damping * rhs_ref[...]
    image_ref[...] = image
    alpha = norm / (both(row_squares(x_ref[...])) + damping * norm)
    residual = rhs_ref[...] - alpha * image
    residual_ref[...] = residual
    scalar_ref[...] = tail(norm, damping, alpha)
    project(residual_ref, f1, s1, ((down[0], down[1]), (down[2], down[3])), tail(row_squares(residual)), outs, bits)


def last_kernel(bits, *refs):
    pieces, (rhs_ref, before_ref, scalar_ref, image_ref, residual_ref, *turned), refs = refs[:4], refs[4:13], refs[13:]
    keep_ref, give_ref, x_ref, ends_ref, y_ref, f0, s0 = refs
    collect(pieces, x_ref, ends_ref, bits)
    following = both(ends_ref[:, 0:1])
    norm = scalar_ref[:, 0:1]
    damping = scalar_ref[:, 1:2]
    alpha = scalar_ref[:, 2:3]
    beta = following / norm
    apply_down(x_ref, f0, s0, (turned[0:2], turned[2:4]), y_ref)
    residual = residual_ref[...]
    image = y_ref[...] + beta * image_ref[...] + damping * residual
    curvature = both(row_squares(x_ref[...] + beta * before_ref[...])) + damping * (following + beta * following)
    alpha_next = following / curvature
    rhs = rhs_ref[...]
    found = alpha * rhs + alpha_next * (residual + beta * rhs)
    left = residual - alpha_next * image
    rows = turned[0].shape[2]
    keep_ref[0] = found[:, :rows]
    keep_ref[1] = left[:, :rows]
    give_ref[0] = found[:, rows:]
    give_ref[1] = left[:, rows:]


def body(down_spectra, up_sources, *, count, receivers):
    me = lax.axis_index("rcv")
    chip_bits = list(range(1, count.bit_length() - 1))
    orders = (chip_bits, chip_bits[::-1])
    ends = (chip_bits[0], chip_bits[-1])
    rows, shots = down_spectra.shape[1:]
    own = up_sources.shape[1] // GROUPS
    chips = count // 2
    packed = 2 * chips * own
    front = shots // 2

    def swap(value, bit):
        return lax.ppermute(value, "rcv", [(at, at ^ (1 << bit)) for at in range(count)])

    def gather(block, order):
        block = block.reshape((1,) * len(chip_bits) + block.shape)
        for bit in order:
            axis = len(chip_bits) - bit
            other = swap(block, bit)
            upper = ((me >> bit) & 1) == 1
            block = jnp.concatenate([jnp.where(upper, other, block), jnp.where(upper, block, other)], axis=axis)
        return block.reshape((-1, shots))

    def exchange(outs):
        pieces = []
        for order, (keep, give) in zip(orders, (outs[0:2], outs[2:4])):
            keep = keep + swap(give, order[0])
            for bit in order[1:]:
                keep = keep + swap(keep, bit)
            pieces += [keep, swap(keep, order[0])]
        return pieces

    other_down = swap(down_spectra, 0)
    sources = []
    for group in range(GROUPS):
        part = up_sources[:, group * own : (group + 1) * own]
        sources.append((gather(part[0], orders[0]), gather(part[1], orders[1])))
    plain_a, turned_a, energy_a = split(down_spectra)
    plain_b, turned_b, energy_b = split(other_down)
    turned = (*turned_a, *turned_b)
    down = (*plain_a, *plain_b, *turned)

    wide = [((2 * packed, shots), bf16)] * 2
    short = [((2 * packed, 2 * rows), bf16)] * 2
    lines = ((packed, 2 * rows), f32)
    every = ((packed, shots), f32)
    small = ((packed, LANES), f32)
    halves = [((packed // 2, front + LANES), f32)] * 2 + [((packed // 2, front), f32)] * 2

    outs = [
        call(functools.partial(rhs_kernel, ends), [lines] + halves, (*pair, *down, energy_a, energy_b), [every] + wide + short)
        for pair in sources
    ]
    rhs = [out[0] for out in outs]
    sums = [exchange(out[1:]) for out in outs]
    outs = [
        call(
            functools.partial(first_kernel, ends, receivers),
            [every, small, lines, lines] + halves,
            (*sums[group], rhs[group], *down),
            [small] + wide + short,
        )
        for group in range(GROUPS)
    ]
    sums = [exchange(out[4:]) for out in outs]
    results = []
    for group in range(GROUPS):
        keep, give = call(
            functools.partial(last_kernel, ends),
            [((2, packed, rows), f32)] * 2,
            (*sums[group], rhs[group], *outs[group][:4], *turned),
            [every, small, lines] + wide,
        )
        results.append((keep, swap(give, 0)))

    upper = (me & 1) == 1

    def order(first, second):
        parts = [jnp.stack([value.reshape(2, 2, chips, own, rows) for value in pair], axis=3) for pair in zip(first, second)]
        return jnp.stack(parts, axis=4).reshape(2, 2, -1, rows).transpose(0, 1, 3, 2)

    found = order(
        [jnp.where(upper, other, keep) for keep, other in results],
        [jnp.where(upper, keep, other) for keep, other in results],
    )
    return found[0], found[1]


def solution(mesh):
    count = mesh.shape["rcv"]

    def run(down_spectra, up_sources):
        return body(down_spectra, up_sources, count=count, receivers=down_spectra.shape[1] * count)

    specs = (P("cuts", "rcv", None), P("cuts", "rcv", None))
    return jax.shard_map(run, mesh=mesh, in_specs=specs, out_specs=specs, check_vma=False)
```

```python
import functools
import jax
import jax.numpy as jnp
from jax import lax
from jax.experimental import pallas as pl
from jax.experimental.pallas import tpu as pltpu
from jax.sharding import PartitionSpec as P

damping_ratio = 0.1
LANES = 128
GROUPS = 2
f32 = jnp.float32
bf16 = jnp.bfloat16


def dot(left, right):
    return lax.dot_general(left, right, (((1,), (0,)), ((), ())), preferred_element_type=f32)


def parts_of(value):
    high = value.astype(bf16)
    return high, (value - high.astype(f32)).astype(bf16)


def call(kernel, outs, args, scratch=(), flops=0, grid=(), in_specs=None):
    spec = pl.BlockSpec(memory_space=pltpu.VMEM)
    moved = sum(value.size * value.dtype.itemsize for value in args)
    return pl.pallas_call(
        kernel,
        out_shape=[jax.ShapeDtypeStruct(shape, dtype) for shape, dtype in outs],
        grid=grid,
        in_specs=in_specs or [spec] * len(args),
        out_specs=[spec] * len(outs),
        scratch_shapes=[pltpu.VMEM(shape, dtype) for shape, dtype in scratch],
        cost_estimate=pl.CostEstimate(flops=flops, transcendentals=0, bytes_accessed=moved),
        compiler_params=pltpu.CompilerParams(vmem_limit_bytes=16 << 20),
    )(*args)


def split_kernel(down_ref, high_ref, low_ref, turned_high_ref, turned_low_ref, energy_ref):
    rows, width = down_ref.shape[1:]
    step = pl.program_id(0)

    @pl.when(step == 0)
    def _():
        energy_ref[...] = jnp.zeros_like(energy_ref)

    at = pl.ds(pl.multiple_of(step * width, width), width)
    for part in range(2):
        value = down_ref[part]
        high, low = parts_of(value)
        high_ref[part, :, at] = high
        low_ref[part, :, at] = low
        turned_high_ref[part, at, :] = high.T
        turned_low_ref[part, at, :] = low.T
        square = jnp.sum((value * value).reshape(rows // 8, 8, width), axis=0)
        energy_ref[...] += sum(square[:, lane : lane + LANES] for lane in range(0, width, LANES))


def split(value):
    _, rows, shots = value.shape
    width = 4 * LANES
    plain, turned = ((2, rows, shots), bf16), ((2, shots, rows), bf16)
    high, low, turned_high, turned_low, energy = call(
        split_kernel,
        [plain, plain, turned, turned, ((8, LANES), f32)],
        (value,),
        grid=(shots // width,),
        in_specs=[pl.BlockSpec((2, rows, width), lambda step: (0, 0, step))],
    )
    return (high, low), (turned_high, turned_low), energy


def stage(value_ref, first_ref, second_ref, sign):
    half = value_ref.shape[0] // 2
    real = value_ref[:half, :]
    imag = value_ref[half:, :]
    for at, (a, b) in enumerate(zip(parts_of(real), parts_of(imag))):
        base = 2 * half * at
        first_ref[base : base + half, :] = a
        first_ref[base + half : base + 2 * half, :] = b
        second_ref[base : base + half, :] = b if sign > 0 else -b
        second_ref[base + half : base + 2 * half, :] = a if sign < 0 else -a


def times(first, second, high_ref, low_ref, columns=slice(None)):
    count = first.shape[0] // 2
    total = dot(first, high_ref[0, :, columns]) + dot(second, high_ref[1, :, columns])
    low = dot(first[:count], low_ref[0, :, columns]) + dot(second[:count], low_ref[1, :, columns])
    return total[:count] + total[count:] + low


def row_squares(value):
    return jnp.sum(value * value, axis=1, keepdims=True)


def both(value):
    half = value.shape[0] // 2
    total = value[:half] + value[half:]
    return jnp.concatenate([total, total], axis=0)


def tail(*columns):
    lane = lax.broadcasted_iota(jnp.int32, (columns[0].shape[0], LANES), 1)
    out = jnp.zeros(lane.shape, f32)
    for at, column in enumerate(columns):
        out = jnp.where(lane == at, column, out)
    return out


def apply_down(x_ref, first_ref, second_ref, turned, image_ref):
    stage(x_ref, first_ref, second_ref, -1)
    rows = turned[0][0].shape[2]
    for at, (high, low) in enumerate(turned):
        image_ref[:, at * rows : (at + 1) * rows] = times(first_ref[...], second_ref[...], high, low)


def device_bit(bit):
    return (lax.axis_index("rcv") >> bit) & 1


def project(value_ref, first_ref, second_ref, plain, extra, outs, bits):
    stage(value_ref, first_ref, second_ref, 1)
    rows = plain[0][0].shape[1]
    shots = plain[0][0].shape[2]
    half = value_ref.shape[0] // 2
    for at, bit in enumerate(bits):
        columns = slice(at * shots // 2, (at + 1) * shots // 2)
        total = 0.0
        for block, (high, low) in enumerate(plain):
            own = slice(block * rows, (block + 1) * rows)
            total = total + times(first_ref[:, own], second_ref[:, own], high, low, columns)
        pieces = [(slice(0, shots // 2), total)]
        if at == 0:
            pieces.append((slice(shots // 2, shots // 2 + LANES), extra))
        keep_ref, give_ref = outs[2 * at : 2 * at + 2]
        upper = device_bit(bit) == 1
        for place, piece in pieces:
            keep_ref[:, place] = jnp.where(upper, piece[half:], piece[:half])
            give_ref[:, place] = jnp.where(upper, piece[:half], piece[half:])


def collect(pieces, x_ref, ends_ref, bits):
    front = x_ref.shape[1] // 2
    for at, bit in enumerate(bits):
        upper = device_bit(bit)
        for which, piece in enumerate(pieces[2 * at : 2 * at + 2]):
            half = piece.shape[0]
            place = pl.ds(pl.multiple_of((upper ^ which) * half, half), half)
            x_ref[place, at * front : (at + 1) * front] = piece[:, :front]
            if at == 0:
                ends_ref[place, :] = piece[:, front:]


def rhs_kernel(bits, masks, *refs):
    sources, refs = refs[:4], refs[4:]
    down, refs = refs[:8], refs[8:]
    (ea, eb), (rhs_ref, *outs), (x_ref, f0, s0, f1, s1, *spread) = refs[:2], refs[2:7], refs[7:]
    half = x_ref.shape[0] // 2
    own = sources[0].shape[1]
    chip = lax.axis_index("rcv") >> 1
    for part in range(2):
        blocks = [ref[at] for ref in sources[2 * part : 2 * part + 2] for at in range(ref.shape[0])]
        for mask, block in zip(masks[part], blocks):
            value = block if part == 0 else -block
            if spread:
                spread[0][part * half // own + (chip ^ mask)] = value
            else:
                x_ref[pl.ds(pl.multiple_of(part * half + (chip ^ mask) * own, own), own), :] = value
    for at in range(2 * half // own if spread else 0):
        x_ref[at * own : (at + 1) * own, :] = spread[0][at]
    apply_down(x_ref, f0, s0, ((down[4], down[5]), (down[6], down[7])), rhs_ref)
    energy = jnp.full((2 * half, 1), jnp.sum(ea[...] + eb[...]), f32)
    extra = tail(row_squares(rhs_ref[...]), energy)
    project(rhs_ref, f1, s1, ((down[0], down[1]), (down[2], down[3])), extra, outs, bits)


def first_kernel(bits, receivers, *refs):
    pieces, (rhs_ref, *refs) = refs[:4], refs[4:]
    down, refs = refs[:8], refs[8:]
    (x_ref, scalar_ref, image_ref, residual_ref, *outs), (ends_ref, f0, s0, f1, s1) = refs[:8], refs[8:]
    collect(pieces, x_ref, ends_ref, bits)
    norm = both(ends_ref[:, 0:1])
    damping = damping_ratio * ends_ref[:, 1:2] / receivers
    apply_down(x_ref, f0, s0, ((down[4], down[5]), (down[6], down[7])), image_ref)
    image = image_ref[...] + damping * rhs_ref[...]
    image_ref[...] = image
    alpha = norm / (both(row_squares(x_ref[...])) + damping * norm)
    residual = rhs_ref[...] - alpha * image
    residual_ref[...] = residual
    scalar_ref[...] = tail(norm, damping, alpha)
    project(residual_ref, f1, s1, ((down[0], down[1]), (down[2], down[3])), tail(row_squares(residual)), outs, bits)


def last_kernel(bits, *refs):
    pieces, (rhs_ref, before_ref, scalar_ref, image_ref, residual_ref, *turned), refs = refs[:4], refs[4:13], refs[13:]
    keep_ref, give_ref, x_ref, ends_ref, y_ref, f0, s0 = refs
    collect(pieces, x_ref, ends_ref, bits)
    following = both(ends_ref[:, 0:1])
    norm = scalar_ref[:, 0:1]
    damping = scalar_ref[:, 1:2]
    alpha = scalar_ref[:, 2:3]
    beta = following / norm
    apply_down(x_ref, f0, s0, (turned[0:2], turned[2:4]), y_ref)
    residual = residual_ref[...]
    image = y_ref[...] + beta * image_ref[...] + damping * residual
    curvature = both(row_squares(x_ref[...] + beta * before_ref[...])) + damping * (following + beta * following)
    alpha_next = following / curvature
    rhs = rhs_ref[...]
    found = alpha * rhs + alpha_next * (residual + beta * rhs)
    left = residual - alpha_next * image
    rows = turned[0].shape[2]
    keep_ref[0] = found[:, :rows]
    keep_ref[1] = left[:, :rows]
    give_ref[0] = found[:, rows:]
    give_ref[1] = left[:, rows:]


def order_kernel(own, *refs):
    pieces, (*outs, x_ref) = refs[: 2 * GROUPS], refs[2 * GROUPS :]
    upper = device_bit(0) == 1
    chips = pieces[0].shape[1] // (2 * own)
    for which, out_ref in enumerate(outs):
        for part in range(2):
            for chip in range(chips):
                source = pl.ds((part * chips + chip) * own, own)
                for group in range(GROUPS):
                    mine = pieces[2 * group][which, source, :]
                    other = pieces[2 * group + 1][which, source, :]
                    base = (2 * chip * GROUPS + group) * own
                    x_ref[base : base + own, :] = jnp.where(upper, other, mine)
                    base += GROUPS * own
                    x_ref[base : base + own, :] = jnp.where(upper, mine, other)
            out_ref[part] = x_ref[...].T


def body(down_spectra, up_sources, *, count, receivers):
    chip_bits = list(range(1, count.bit_length() - 1))
    orders = (chip_bits, chip_bits[::-1])
    ends = (chip_bits[0], chip_bits[-1])
    rows, shots = down_spectra.shape[1:]
    own = up_sources.shape[1] // GROUPS
    chips = count // 2
    packed = 2 * chips * own
    front = shots // 2

    def swap(value, bit):
        return lax.ppermute(value, "rcv", [(at, at ^ (1 << bit)) for at in range(count)])

    def gather(block, order):
        blocks, masks = block[None], [0]
        for bit in order[:-1]:
            blocks = jnp.concatenate([blocks, swap(blocks, bit)], axis=0)
            masks += [mask | 1 << bit - 1 for mask in masks]
        return (blocks, swap(blocks, order[-1])), masks + [mask | 1 << order[-1] - 1 for mask in masks]

    def exchange(outs):
        pieces = []
        for order, (keep, give) in zip(orders, (outs[0:2], outs[2:4])):
            keep = keep + swap(give, order[0])
            for bit in order[1:]:
                keep = keep + swap(keep, bit)
            pieces += [keep, swap(keep, order[0])]
        return pieces

    other_down = swap(down_spectra, 0)
    sources = []
    for group in range(GROUPS):
        part = up_sources[:, group * own : (group + 1) * own]
        (real, real_masks), (imag, imag_masks) = gather(part[0], orders[0]), gather(part[1], orders[1])
        sources.append((*real, *imag))
    masks = (real_masks, imag_masks)
    plain_a, turned_a, energy_a = split(down_spectra)
    plain_b, turned_b, energy_b = split(other_down)
    turned = (*turned_a, *turned_b)
    down = (*plain_a, *plain_b, *turned)

    wide = [((2 * packed, shots), bf16)] * 2
    short = [((2 * packed, 2 * rows), bf16)] * 2
    lines = ((packed, 2 * rows), f32)
    every = ((packed, shots), f32)
    small = ((packed, LANES), f32)
    work = 2 * 2 * 2 * (3 * packed) * 2 * rows * shots
    halves = [((packed // 2, front + LANES), f32)] * 2 + [((packed // 2, front), f32)] * 2

    spread = [((packed // own, own, shots), f32)] if own % 8 else []
    outs = [
        call(
            functools.partial(rhs_kernel, ends, masks),
            [lines] + halves,
            (*pair, *down, energy_a, energy_b),
            [every] + wide + short + spread,
            work,
        )
        for pair in sources
    ]
    rhs = [out[0] for out in outs]
    sums = [exchange(out[1:]) for out in outs]
    outs = [
        call(
            functools.partial(first_kernel, ends, receivers),
            [every, small, lines, lines] + halves,
            (*sums[group], rhs[group], *down),
            [small] + wide + short,
            work,
        )
        for group in range(GROUPS)
    ]
    sums = [exchange(out[4:]) for out in outs]
    results = []
    for group in range(GROUPS):
        keep, give = call(
            functools.partial(last_kernel, ends),
            [((2, packed, rows), f32)] * 2,
            (*sums[group], rhs[group], *outs[group][:4], *turned),
            [every, small, lines] + wide,
            work // 2,
        )
        results.append((keep, swap(give, 0)))

    pieces = [piece for pair in results for piece in pair]
    columns = GROUPS * packed
    return tuple(call(functools.partial(order_kernel, own), [((2, rows, columns), f32)] * 2, pieces, [((columns, rows), f32)]))


def solution(mesh):
    count = mesh.shape["rcv"]

    def run(down_spectra, up_sources):
        return body(down_spectra, up_sources, count=count, receivers=down_spectra.shape[1] * count)

    specs = (P("cuts", "rcv", None), P("cuts", "rcv", None))
    return jax.shard_map(run, mesh=mesh, in_specs=specs, out_specs=specs, check_vma=False)
```

```python
import functools
import jax
import jax.numpy as jnp
from jax import lax
from jax.experimental import pallas as pl
from jax.experimental.pallas import tpu as pltpu
from jax.sharding import PartitionSpec as P

damping_ratio = 0.1
LANES = 128
GROUPS = 2
f32 = jnp.float32
bf16 = jnp.bfloat16


def dot(left, right):
    return lax.dot_general(left, right, (((1,), (0,)), ((), ())), preferred_element_type=f32)


def parts_of(value):
    high = value.astype(bf16)
    return high, (value - high.astype(f32)).astype(bf16)


def call(kernel, outs, args, scratch=(), flops=0, grid=(), in_specs=None):
    spec = pl.BlockSpec(memory_space=pltpu.VMEM)
    moved = sum(value.size * value.dtype.itemsize for value in args)
    return pl.pallas_call(
        kernel,
        out_shape=[jax.ShapeDtypeStruct(shape, dtype) for shape, dtype in outs],
        grid=grid,
        in_specs=in_specs or [spec] * len(args),
        out_specs=[spec] * len(outs),
        scratch_shapes=[pltpu.VMEM(shape, dtype) for shape, dtype in scratch],
        cost_estimate=pl.CostEstimate(flops=flops, transcendentals=0, bytes_accessed=moved),
        compiler_params=pltpu.CompilerParams(vmem_limit_bytes=16 << 20),
    )(*args)


def split_kernel(down_ref, high_ref, low_ref, turned_high_ref, turned_low_ref, energy_ref):
    rows, width = down_ref.shape[1:]
    step = pl.program_id(0)

    @pl.when(step == 0)
    def _():
        energy_ref[...] = jnp.zeros_like(energy_ref)

    at = pl.ds(pl.multiple_of(step * width, width), width)
    for part in range(2):
        value = down_ref[part]
        high, low = parts_of(value)
        high_ref[part, :, at] = high
        low_ref[part, :, at] = low
        turned_high_ref[part, at, :] = high.T
        turned_low_ref[part, at, :] = low.T
        square = jnp.sum((value * value).reshape(rows // 8, 8, width), axis=0)
        energy_ref[...] += sum(square[:, lane : lane + LANES] for lane in range(0, width, LANES))


def split(value):
    _, rows, shots = value.shape
    width = 4 * LANES
    plain, turned = ((2, rows, shots), bf16), ((2, shots, rows), bf16)
    high, low, turned_high, turned_low, energy = call(
        split_kernel,
        [plain, plain, turned, turned, ((8, LANES), f32)],
        (value,),
        grid=(shots // width,),
        in_specs=[pl.BlockSpec((2, rows, width), lambda step: (0, 0, step))],
    )
    return (high, low), (turned_high, turned_low), energy


def stage(value_ref, first_ref, second_ref, sign):
    half = value_ref.shape[0] // 2
    real = value_ref[:half, :]
    imag = value_ref[half:, :]
    for at, (a, b) in enumerate(zip(parts_of(real), parts_of(imag))):
        base = 2 * half * at
        first_ref[base : base + half, :] = a
        first_ref[base + half : base + 2 * half, :] = b
        second_ref[base : base + half, :] = b if sign > 0 else -b
        second_ref[base + half : base + 2 * half, :] = a if sign < 0 else -a


def times(first, second, high_ref, low_ref, columns=slice(None)):
    count = first.shape[0] // 2
    total = dot(first, high_ref[0, :, columns]) + dot(second, high_ref[1, :, columns])
    low = dot(first[:count], low_ref[0, :, columns]) + dot(second[:count], low_ref[1, :, columns])
    return total[:count] + total[count:] + low


def row_squares(value):
    return jnp.sum(value * value, axis=1, keepdims=True)


def both(value):
    half = value.shape[0] // 2
    total = value[:half] + value[half:]
    return jnp.concatenate([total, total], axis=0)


def tail(*columns):
    lane = lax.broadcasted_iota(jnp.int32, (columns[0].shape[0], LANES), 1)
    out = jnp.zeros(lane.shape, f32)
    for at, column in enumerate(columns):
        out = jnp.where(lane == at, column, out)
    return out


def apply_down(x_ref, first_ref, second_ref, turned, image_ref):
    stage(x_ref, first_ref, second_ref, -1)
    rows = turned[0][0].shape[2]
    for at, (high, low) in enumerate(turned):
        image_ref[:, at * rows : (at + 1) * rows] = times(first_ref[...], second_ref[...], high, low)


def device_bit(bit):
    return (lax.axis_index("rcv") >> bit) & 1


def project(value_ref, first_ref, second_ref, plain, extra, outs, bits):
    stage(value_ref, first_ref, second_ref, 1)
    rows = plain[0][0].shape[1]
    shots = plain[0][0].shape[2]
    half = value_ref.shape[0] // 2
    for at, bit in enumerate(bits):
        columns = slice(at * shots // 2, (at + 1) * shots // 2)
        total = 0.0
        for block, (high, low) in enumerate(plain):
            own = slice(block * rows, (block + 1) * rows)
            total = total + times(first_ref[:, own], second_ref[:, own], high, low, columns)
        pieces = [(slice(0, shots // 2), total)]
        if at == 0:
            pieces.append((slice(shots // 2, shots // 2 + LANES), extra))
        keep_ref, give_ref = outs[2 * at : 2 * at + 2]
        upper = device_bit(bit) == 1
        for place, piece in pieces:
            keep_ref[:, place] = jnp.where(upper, piece[half:], piece[:half])
            give_ref[:, place] = jnp.where(upper, piece[:half], piece[half:])


def collect(pieces, x_ref, ends_ref, bits):
    front = x_ref.shape[1] // 2
    for at, bit in enumerate(bits):
        upper = device_bit(bit)
        for which, piece in enumerate(pieces[2 * at : 2 * at + 2]):
            half = piece.shape[0]
            place = pl.ds(pl.multiple_of((upper ^ which) * half, half), half)
            x_ref[place, at * front : (at + 1) * front] = piece[:, :front]
            if at == 0:
                ends_ref[place, :] = piece[:, front:]


def rhs_kernel(bits, masks, *refs):
    sources, refs = refs[: len(masks)], refs[len(masks) :]
    down, refs = refs[:8], refs[8:]
    (ea, eb), (rhs_ref, *outs), (x_ref, f0, s0, f1, s1, *spread) = refs[:2], refs[2:7], refs[7:]
    half = x_ref.shape[0] // 2
    own = sources[0].shape[1]
    chip = lax.axis_index("rcv") >> 1
    for mask, source in zip(masks, sources):
        for part, value in enumerate((source[0], -source[1])):
            if spread:
                spread[0][part * half // own + (chip ^ mask)] = value
            else:
                x_ref[pl.ds(pl.multiple_of(part * half + (chip ^ mask) * own, own), own), :] = value
    for at in range(2 * half // own if spread else 0):
        x_ref[at * own : (at + 1) * own, :] = spread[0][at]
    apply_down(x_ref, f0, s0, ((down[4], down[5]), (down[6], down[7])), rhs_ref)
    energy = jnp.full((2 * half, 1), jnp.sum(ea[...] + eb[...]), f32)
    extra = tail(row_squares(rhs_ref[...]), energy)
    project(rhs_ref, f1, s1, ((down[0], down[1]), (down[2], down[3])), extra, outs, bits)


def first_kernel(bits, receivers, *refs):
    pieces, (rhs_ref, *refs) = refs[:4], refs[4:]
    down, refs = refs[:8], refs[8:]
    (x_ref, scalar_ref, image_ref, residual_ref, *outs), (ends_ref, f0, s0, f1, s1) = refs[:8], refs[8:]
    collect(pieces, x_ref, ends_ref, bits)
    norm = both(ends_ref[:, 0:1])
    damping = damping_ratio * ends_ref[:, 1:2] / receivers
    apply_down(x_ref, f0, s0, ((down[4], down[5]), (down[6], down[7])), image_ref)
    image = image_ref[...] + damping * rhs_ref[...]
    image_ref[...] = image
    alpha = norm / (both(row_squares(x_ref[...])) + damping * norm)
    residual = rhs_ref[...] - alpha * image
    residual_ref[...] = residual
    scalar_ref[...] = tail(norm, damping, alpha)
    project(residual_ref, f1, s1, ((down[0], down[1]), (down[2], down[3])), tail(row_squares(residual)), outs, bits)


def last_kernel(bits, *refs):
    pieces, (rhs_ref, before_ref, scalar_ref, image_ref, residual_ref, *turned), refs = refs[:4], refs[4:13], refs[13:]
    keep_ref, give_ref, x_ref, ends_ref, y_ref, f0, s0 = refs
    collect(pieces, x_ref, ends_ref, bits)
    following = both(ends_ref[:, 0:1])
    norm = scalar_ref[:, 0:1]
    damping = scalar_ref[:, 1:2]
    alpha = scalar_ref[:, 2:3]
    beta = following / norm
    apply_down(x_ref, f0, s0, (turned[0:2], turned[2:4]), y_ref)
    residual = residual_ref[...]
    image = y_ref[...] + beta * image_ref[...] + damping * residual
    curvature = both(row_squares(x_ref[...] + beta * before_ref[...])) + damping * (following + beta * following)
    alpha_next = following / curvature
    rhs = rhs_ref[...]
    found = alpha * rhs + alpha_next * (residual + beta * rhs)
    left = residual - alpha_next * image
    rows = turned[0].shape[2]
    keep_ref[0] = found[:, :rows]
    keep_ref[1] = left[:, :rows]
    give_ref[0] = found[:, rows:]
    give_ref[1] = left[:, rows:]


def order_kernel(own, *refs):
    pieces, (*outs, x_ref) = refs[: 2 * GROUPS], refs[2 * GROUPS :]
    upper = device_bit(0) == 1
    chips = pieces[0].shape[1] // (2 * own)
    for which, out_ref in enumerate(outs):
        for part in range(2):
            for chip in range(chips):
                source = pl.ds((part * chips + chip) * own, own)
                for group in range(GROUPS):
                    mine = pieces[2 * group][which, source, :]
                    other = pieces[2 * group + 1][which, source, :]
                    base = (2 * chip * GROUPS + group) * own
                    x_ref[base : base + own, :] = jnp.where(upper, other, mine)
                    base += GROUPS * own
                    x_ref[base : base + own, :] = jnp.where(upper, mine, other)
            out_ref[part] = x_ref[...].T


def body(down_spectra, up_sources, *, count, receivers):
    chip_bits = list(range(1, count.bit_length() - 1))
    orders = (chip_bits, chip_bits[::-1])
    ends = (chip_bits[0], chip_bits[-1])
    rows, shots = down_spectra.shape[1:]
    own = up_sources.shape[1] // GROUPS
    chips = count // 2
    packed = 2 * chips * own
    front = shots // 2

    def swap(value, bit):
        return lax.ppermute(value, "rcv", [(at, at ^ (1 << bit)) for at in range(count)])

    def exchange(outs):
        pieces = []
        for order, (keep, give) in zip(orders, (outs[0:2], outs[2:4])):
            keep = keep + swap(give, order[0])
            for bit in order[1:]:
                keep = keep + swap(keep, bit)
            pieces += [keep, swap(keep, order[0])]
        return pieces

    def jump(value, mask):
        return lax.ppermute(value, "rcv", [(at, at ^ (mask << 1)) for at in range(count)])

    other_down = swap(down_spectra, 0)
    masks = sorted(range(chips), key=lambda mask: mask.bit_count())
    sources = []
    for group in range(GROUPS):
        part = up_sources[:, group * own : (group + 1) * own]
        sources.append([jump(part, mask) if mask else part for mask in masks])
    plain_a, turned_a, energy_a = split(pltpu.with_memory_space_constraint(down_spectra, pltpu.HBM))
    plain_b, turned_b, energy_b = split(other_down)
    turned = (*turned_a, *turned_b)
    down = (*plain_a, *plain_b, *turned)

    wide = [((2 * packed, shots), bf16)] * 2
    short = [((2 * packed, 2 * rows), bf16)] * 2
    lines = ((packed, 2 * rows), f32)
    every = ((packed, shots), f32)
    small = ((packed, LANES), f32)
    work = 2 * 2 * 2 * (3 * packed) * 2 * rows * shots
    halves = [((packed // 2, front + LANES), f32)] * 2 + [((packed // 2, front), f32)] * 2

    spread = [((packed // own, own, shots), f32)] if own % 8 else []
    outs = [
        call(
            functools.partial(rhs_kernel, ends, masks),
            [lines] + halves,
            (*pair, *down, energy_a, energy_b),
            [every] + wide + short + spread,
            work,
        )
        for pair in sources
    ]
    rhs = [out[0] for out in outs]
    sums = [exchange(out[1:]) for out in outs]
    outs = [
        call(
            functools.partial(first_kernel, ends, receivers),
            [every, small, lines, lines] + halves,
            (*sums[group], rhs[group], *down),
            [small] + wide + short,
            work,
        )
        for group in range(GROUPS)
    ]
    sums = [exchange(out[4:]) for out in outs]
    results = []
    for group in range(GROUPS):
        keep, give = call(
            functools.partial(last_kernel, ends),
            [((2, packed, rows), f32)] * 2,
            (*sums[group], rhs[group], *outs[group][:4], *turned),
            [every, small, lines] + wide,
            work // 2,
        )
        results.append((keep, swap(give, 0)))

    pieces = [piece for pair in results for piece in pair]
    columns = GROUPS * packed
    return tuple(call(functools.partial(order_kernel, own), [((2, rows, columns), f32)] * 2, pieces, [((columns, rows), f32)]))


def solution(mesh):
    count = mesh.shape["rcv"]

    def run(down_spectra, up_sources):
        return body(down_spectra, up_sources, count=count, receivers=down_spectra.shape[1] * count)

    specs = (P("cuts", "rcv", None), P("cuts", "rcv", None))
    return jax.shard_map(run, mesh=mesh, in_specs=specs, out_specs=specs, check_vma=False)
```

```python
import functools
import jax
import jax.numpy as jnp
from jax import lax
from jax.experimental import pallas as pl
from jax.experimental.pallas import tpu as pltpu
from jax.sharding import PartitionSpec as P

damping_ratio = 0.1
LANES = 128
GROUPS = 2
f32 = jnp.float32
bf16 = jnp.bfloat16


def dot(left, right):
    return lax.dot_general(left, right, (((1,), (0,)), ((), ())), preferred_element_type=f32)


def parts_of(value):
    high = value.astype(bf16)
    return high, (value - high.astype(f32)).astype(bf16)


def call(kernel, outs, args, scratch=(), flops=0, grid=(), in_specs=None):
    spec = pl.BlockSpec(memory_space=pltpu.VMEM)
    moved = sum(value.size * value.dtype.itemsize for value in args)
    return pl.pallas_call(
        kernel,
        out_shape=[jax.ShapeDtypeStruct(shape, dtype) for shape, dtype in outs],
        grid=grid,
        in_specs=in_specs or [spec] * len(args),
        out_specs=[spec] * len(outs),
        scratch_shapes=[pltpu.VMEM(shape, dtype) for shape, dtype in scratch],
        cost_estimate=pl.CostEstimate(flops=flops, transcendentals=0, bytes_accessed=moved),
        compiler_params=pltpu.CompilerParams(vmem_limit_bytes=16 << 20),
    )(*args)


def split_kernel(down_ref, high_ref, low_ref, turned_high_ref, turned_low_ref, energy_ref):
    rows, shots = down_ref.shape[1:]
    part, step = pl.program_id(0), pl.program_id(1)
    width = 4 * LANES
    whole = rows == high_ref.shape[1]
    at = slice(None) if whole else pl.ds(pl.multiple_of(step * rows, rows), rows)

    @pl.when((part == 0) & (step == 0))
    def _():
        energy_ref[...] = jnp.zeros_like(energy_ref)

    for start in range(0, shots, width):
        place = slice(start, start + width)
        value = down_ref[0, :, place]
        high, low = parts_of(value)
        high_ref[part, at, place] = high
        low_ref[part, at, place] = low
        turned_high_ref[part, place, at] = high.T
        turned_low_ref[part, place, at] = low.T
        square = jnp.sum((value * value).reshape(rows // 8, 8, width), axis=0)
        energy_ref[...] += sum(square[:, lane : lane + LANES] for lane in range(0, width, LANES))


def split(value):
    _, rows, shots = value.shape
    block = min(rows, LANES)
    plain, turned = ((2, rows, shots), bf16), ((2, shots, rows), bf16)
    high, low, turned_high, turned_low, energy = call(
        split_kernel,
        [plain, plain, turned, turned, ((8, LANES), f32)],
        (value,),
        grid=(2, rows // block),
        in_specs=[pl.BlockSpec((1, block, shots), lambda part, step: (part, step, 0))],
    )
    return (high, low), (turned_high, turned_low), energy


def stage(value_ref, first_ref, second_ref, sign):
    half = value_ref.shape[0] // 2
    real = value_ref[:half, :]
    imag = value_ref[half:, :]
    for at, (a, b) in enumerate(zip(parts_of(real), parts_of(imag))):
        base = 2 * half * at
        first_ref[base : base + half, :] = a
        first_ref[base + half : base + 2 * half, :] = b
        second_ref[base : base + half, :] = b if sign > 0 else -b
        second_ref[base + half : base + 2 * half, :] = a if sign < 0 else -a


def times(first, second, high_ref, low_ref, columns=slice(None)):
    count = first.shape[0] // 2
    total = dot(first, high_ref[0, :, columns]) + dot(second, high_ref[1, :, columns])
    low = dot(first[:count], low_ref[0, :, columns]) + dot(second[:count], low_ref[1, :, columns])
    return total[:count] + total[count:] + low


def row_squares(value):
    return jnp.sum(value * value, axis=1, keepdims=True)


def both(value):
    half = value.shape[0] // 2
    total = value[:half] + value[half:]
    return jnp.concatenate([total, total], axis=0)


def tail(*columns):
    lane = lax.broadcasted_iota(jnp.int32, (columns[0].shape[0], LANES), 1)
    out = jnp.zeros(lane.shape, f32)
    for at, column in enumerate(columns):
        out = jnp.where(lane == at, column, out)
    return out


def apply_down(x_ref, first_ref, second_ref, turned, shots=slice(None)):
    stage(x_ref, first_ref, second_ref, -1)
    first, second = first_ref[...], second_ref[...]
    count = first.shape[0] // 2
    blocks = []
    for high, low in turned:
        total = dot(first, high[0, shots, :]) + dot(second, high[1, shots, :])
        rest = dot(first[:count], low[0, shots, :]) + dot(second[:count], low[1, shots, :])
        blocks.append(total[:count] + total[count:] + rest)
    return jnp.concatenate(blocks, axis=1)


def device_bit(bit):
    return (lax.axis_index("rcv") >> bit) & 1


def project(value_ref, first_ref, second_ref, plain, columns, keep_ref, give_ref, bit, extra=None):
    stage(value_ref, first_ref, second_ref, 1)
    rows = plain[0][0].shape[1]
    half = value_ref.shape[0] // 2
    front = columns.stop - columns.start
    total = 0.0
    for block, (high, low) in enumerate(plain):
        own = slice(block * rows, (block + 1) * rows)
        total = total + times(first_ref[:, own], second_ref[:, own], high, low, columns)
    upper = device_bit(bit) == 1
    keep_ref[:, :front] = jnp.where(upper, total[half:], total[:half])
    give_ref[:, :front] = jnp.where(upper, total[:half], total[half:])
    if extra is not None:
        keep_ref[:, front:] = jnp.where(upper, extra[half:], extra[:half])
        give_ref[:, front:] = jnp.where(upper, extra[:half], extra[half:])


def collect(pieces, x_ref, bit, ends_ref=None):
    upper = device_bit(bit)
    front = x_ref.shape[1]
    for which, piece in enumerate(pieces):
        half = piece.shape[0]
        place = pl.ds(pl.multiple_of((upper ^ which) * half, half), half)
        x_ref[place, :] = piece[:, :front]
        if ends_ref is not None:
            ends_ref[place, :] = piece[:, front:]


def pairs(refs):
    return tuple((refs[at], refs[at + 1]) for at in range(0, len(refs), 2))


def rhs_kernel(bit, masks, *refs):
    sources, refs = refs[: len(masks)], refs[len(masks) :]
    down, refs = refs[:8], refs[8:]
    (ea, eb), (rhs_ref, *outs), (x_ref, f0, s0, f1, s1, *spread) = refs[:2], refs[2:5], refs[5:]
    half = x_ref.shape[0] // 2
    own = sources[0].shape[1]
    chip = lax.axis_index("rcv") >> 1
    for mask, source in zip(masks, sources):
        for part, value in enumerate((source[0], -source[1])):
            if spread:
                spread[0][part * half // own + (chip ^ mask)] = value
            else:
                x_ref[pl.ds(pl.multiple_of(part * half + (chip ^ mask) * own, own), own), :] = value
    for at in range(2 * half // own if spread else 0):
        x_ref[at * own : (at + 1) * own, :] = spread[0][at]
    rhs_ref[...] = apply_down(x_ref, f0, s0, pairs(down[4:]))
    energy = jnp.full((2 * half, 1), jnp.sum(ea[...] + eb[...]), f32)
    extra = tail(row_squares(rhs_ref[...]), energy)
    front = outs[0].shape[1] - LANES
    project(rhs_ref, f1, s1, pairs(down[:4]), slice(0, front), *outs, bit, extra)


def back_kernel(bit, *refs):
    value_ref, down, outs, scratch = refs[0], refs[1:5], refs[5:7], refs[7:]
    shots = down[0].shape[2]
    project(value_ref, *scratch, pairs(down), slice(shots - outs[0].shape[1], shots), *outs, bit)


def front_kernel(bit, *refs):
    pieces, turned, (x_ref, ends_ref, image_ref), scratch = refs[:2], refs[2:6], refs[6:9], refs[9:]
    collect(pieces, x_ref, bit, ends_ref)
    image_ref[...] = apply_down(x_ref, *scratch, pairs(turned), slice(0, x_ref.shape[1]))


def first_kernel(bits, receivers, *refs):
    pieces, (before_ref, ends_ref, part_ref, rhs_ref, *refs) = refs[:2], refs[2:]
    down, refs = refs[:8], refs[8:]
    (x_ref, scalar_ref, image_ref, residual_ref, *outs), (f0, s0, f1, s1) = refs[:6], refs[6:]
    front = before_ref.shape[1]
    collect(pieces, x_ref, bits[1])
    norm = both(ends_ref[:, 0:1])
    damping = damping_ratio * ends_ref[:, 1:2] / receivers
    image = part_ref[...] + apply_down(x_ref, f0, s0, pairs(down[4:]), slice(front, None)) + damping * rhs_ref[...]
    image_ref[...] = image
    alpha = norm / (both(row_squares(before_ref[...]) + row_squares(x_ref[...])) + damping * norm)
    residual = rhs_ref[...] - alpha * image
    residual_ref[...] = residual
    scalar_ref[...] = tail(norm, damping, alpha)
    project(residual_ref, f1, s1, pairs(down[:4]), slice(0, front), *outs, bits[0], tail(row_squares(residual)))


def last_kernel(bit, *refs):
    pieces, (a_ref, ends_ref, part_ref, rhs_ref, before_a, before_b, scalar_ref, image_ref, residual_ref) = refs[:2], refs[2:11]
    turned, (keep_ref, give_ref, x_ref, *scratch) = refs[11:15], refs[15:]
    front = a_ref.shape[1]
    collect(pieces, x_ref, bit)
    following = both(ends_ref[:, 0:1])
    norm = scalar_ref[:, 0:1]
    damping = scalar_ref[:, 1:2]
    alpha = scalar_ref[:, 2:3]
    beta = following / norm
    residual = residual_ref[...]
    image = part_ref[...] + apply_down(x_ref, *scratch, pairs(turned), slice(front, None))
    image = image + beta * image_ref[...] + damping * residual
    squares = row_squares(a_ref[...] + beta * before_a[...]) + row_squares(x_ref[...] + beta * before_b[...])
    curvature = both(squares) + damping * (following + beta * following)
    alpha_next = following / curvature
    rhs = rhs_ref[...]
    found = alpha * rhs + alpha_next * (residual + beta * rhs)
    left = residual - alpha_next * image
    rows = turned[0].shape[2]
    keep_ref[0] = found[:, :rows]
    keep_ref[1] = left[:, :rows]
    give_ref[0] = found[:, rows:]
    give_ref[1] = left[:, rows:]


def order_kernel(own, *refs):
    pieces, (*outs, x_ref) = refs[: 2 * GROUPS], refs[2 * GROUPS :]
    upper = device_bit(0) == 1
    chips = pieces[0].shape[1] // (2 * own)
    for which, out_ref in enumerate(outs):
        for part in range(2):
            for chip in range(chips):
                source = pl.ds((part * chips + chip) * own, own)
                for group in range(GROUPS):
                    mine = pieces[2 * group][which, source, :]
                    other = pieces[2 * group + 1][which, source, :]
                    base = (2 * chip * GROUPS + group) * own
                    x_ref[base : base + own, :] = jnp.where(upper, other, mine)
                    base += GROUPS * own
                    x_ref[base : base + own, :] = jnp.where(upper, mine, other)
            out_ref[part] = x_ref[...].T


def body(down_spectra, up_sources, *, count, receivers):
    chip_bits = list(range(1, count.bit_length() - 1))
    orders = (chip_bits, chip_bits[::-1])
    ends = (chip_bits[0], chip_bits[-1])
    rows, shots = down_spectra.shape[1:]
    own = up_sources.shape[1] // GROUPS
    chips = count // 2
    packed = 2 * chips * own
    front = shots // 2

    def swap(value, bit):
        return lax.ppermute(value, "rcv", [(at, at ^ (1 << bit)) for at in range(count)])

    def exchange(*ranges):
        pieces = []
        for order, (keep, give) in zip(orders, ranges):
            keep = keep + swap(give, order[0])
            for bit in order[1:]:
                keep = keep + swap(keep, bit)
            pieces.append((keep, swap(keep, order[0])))
        return pieces

    def jump(value, mask):
        return lax.ppermute(value, "rcv", [(at, at ^ (mask << 1)) for at in range(count)])

    other_down = swap(down_spectra, 0)
    masks = sorted(range(chips), key=lambda mask: mask.bit_count())
    sources = []
    for group in range(GROUPS):
        part = up_sources[:, group * own : (group + 1) * own]
        sources.append([jump(part, mask) if mask else part for mask in masks])
    plain_a, turned_a, energy_a = split(pltpu.with_memory_space_constraint(down_spectra, pltpu.HBM))
    plain_b, turned_b, energy_b = split(other_down)
    turned = (*turned_a, *turned_b)
    down = (*plain_a, *plain_b, *turned)

    wide = [((2 * packed, shots), bf16)] * 2
    narrow = [((2 * packed, front), bf16)] * 2
    short = [((2 * packed, 2 * rows), bf16)] * 2
    lines = ((packed, 2 * rows), f32)
    every = ((packed, shots), f32)
    ranged = ((packed, front), f32)
    small = ((packed, LANES), f32)
    work = 2 * 2 * 2 * (3 * packed) * rows * shots
    sent_0 = [((packed // 2, front + LANES), f32)] * 2
    sent_1 = [((packed // 2, front), f32)] * 2
    spread = [((packed // own, own, shots), f32)] if own % 8 else []
    plain = (*plain_a, *plain_b)

    def back(value):
        return call(functools.partial(back_kernel, ends[1]), sent_1, (value, *plain), short, work)

    def lead(pieces):
        return call(functools.partial(front_kernel, ends[0]), [ranged, small, lines], (*pieces, *turned), narrow, work)

    state, sums = [], []
    for source in sources:
        rhs, *outs = call(
            functools.partial(rhs_kernel, ends[0], masks),
            [lines] + sent_0,
            (*source, *down, energy_a, energy_b),
            [every] + wide + short + spread,
            3 * work,
        )
        state.append(rhs)
        sums.append(exchange(outs, back(rhs)))
    for group, (rhs, (pieces_0, pieces_1)) in enumerate(zip(state, sums)):
        before, norms, part = lead(pieces_0)
        x, scalars, image, residual, *outs = call(
            functools.partial(first_kernel, ends, receivers),
            [ranged, small, lines, lines] + sent_0,
            (*pieces_1, before, norms, part, rhs, *down),
            narrow + short,
            2 * work,
        )
        state[group] = (rhs, before, x, scalars, image, residual)
        sums[group] = exchange(outs, back(residual))
    results = []
    for kept, (pieces_0, pieces_1) in zip(state, sums):
        keep, give = call(
            functools.partial(last_kernel, ends[1]),
            [((2, packed, rows), f32)] * 2,
            (*pieces_1, *lead(pieces_0), *kept, *turned),
            [ranged] + narrow,
            work,
        )
        results.append((keep, swap(give, 0)))

    pieces = [piece for pair in results for piece in pair]
    columns = GROUPS * packed
    return tuple(call(functools.partial(order_kernel, own), [((2, rows, columns), f32)] * 2, pieces, [((columns, rows), f32)]))


def solution(mesh):
    count = mesh.shape["rcv"]

    def run(down_spectra, up_sources):
        return body(down_spectra, up_sources, count=count, receivers=down_spectra.shape[1] * count)

    specs = (P("cuts", "rcv", None), P("cuts", "rcv", None))
    return jax.shard_map(run, mesh=mesh, in_specs=specs, out_specs=specs, check_vma=False)
```

```python
import functools
import jax
import jax.numpy as jnp
from jax import lax
from jax.experimental import pallas as pl
from jax.experimental.pallas import tpu as pltpu
from jax.sharding import PartitionSpec as P

damping_ratio = 0.1
LANES = 128
GROUPS = 2
f32 = jnp.float32
bf16 = jnp.bfloat16


def dot(left, right):
    return lax.dot_general(left, right, (((1,), (0,)), ((), ())), preferred_element_type=f32)


def parts_of(value):
    high = value.astype(bf16)
    return high, (value - high.astype(f32)).astype(bf16)


def call(kernel, outs, args, scratch=(), flops=0, grid=(), in_specs=None):
    spec = pl.BlockSpec(memory_space=pltpu.VMEM)
    moved = sum(value.size * value.dtype.itemsize for value in args)
    return pl.pallas_call(
        kernel,
        out_shape=[jax.ShapeDtypeStruct(shape, dtype) for shape, dtype in outs],
        grid=grid,
        in_specs=in_specs or [spec] * len(args),
        out_specs=[spec] * len(outs),
        scratch_shapes=[pltpu.VMEM(shape, dtype) for shape, dtype in scratch],
        cost_estimate=pl.CostEstimate(flops=flops, transcendentals=0, bytes_accessed=moved),
        compiler_params=pltpu.CompilerParams(vmem_limit_bytes=16 << 20),
    )(*args)


def split_kernel(real_ref, imag_ref, high_ref, low_ref, turned_high_ref, turned_low_ref, energy_ref):
    rows, shots = real_ref.shape[1:]
    step, chunk = pl.program_id(0), pl.program_id(1)
    width = 2 * LANES
    at = slice(None) if rows == high_ref.shape[1] else pl.ds(pl.multiple_of(step * rows, rows), rows)

    @pl.when((step == 0) & (chunk == 0))
    def _():
        energy_ref[...] = jnp.zeros_like(energy_ref)

    for part, ref in enumerate((real_ref, imag_ref)):
        for start in range(0, shots, width):
            value = ref[0, :, start : start + width]
            place = pl.ds(pl.multiple_of(chunk * shots + start, width), width)
            high, low = parts_of(value)
            high_ref[part, at, place] = high
            low_ref[part, at, place] = low
            turned_high_ref[part, place, at] = high.T
            turned_low_ref[part, place, at] = low.T
            square = jnp.sum((value * value).reshape(rows // 8, 8, width), axis=0)
            energy_ref[...] += sum(square[:, lane : lane + LANES] for lane in range(0, width, LANES))


def split(value):
    _, rows, shots = value.shape
    block, chunks = min(rows, LANES), 2
    plain, turned = ((2, rows, shots), bf16), ((2, shots, rows), bf16)
    high, low, turned_high, turned_low, energy = call(
        split_kernel,
        [plain, plain, turned, turned, ((8, LANES), f32)],
        (value, value),
        grid=(rows // block, chunks),
        in_specs=[
            pl.BlockSpec((1, block, shots // chunks), lambda step, chunk: (0, step, chunk)),
            pl.BlockSpec((1, block, shots // chunks), lambda step, chunk: (1, step, chunk)),
        ],
    )
    return (high, low), (turned_high, turned_low), energy


def stage(value_ref, first_ref, second_ref, sign):
    half = value_ref.shape[0] // 2
    real = value_ref[:half, :]
    imag = value_ref[half:, :]
    for at, (a, b) in enumerate(zip(parts_of(real), parts_of(imag))):
        base = 2 * half * at
        first_ref[base : base + half, :] = a
        first_ref[base + half : base + 2 * half, :] = b
        second_ref[base : base + half, :] = b if sign > 0 else -b
        second_ref[base + half : base + 2 * half, :] = a if sign < 0 else -a


def times(first, second, high_ref, low_ref, columns=slice(None)):
    count = first.shape[0] // 2
    total = dot(first, high_ref[0, :, columns]) + dot(second, high_ref[1, :, columns])
    low = dot(first[:count], low_ref[0, :, columns]) + dot(second[:count], low_ref[1, :, columns])
    return total[:count] + total[count:] + low


def row_squares(value):
    return jnp.sum(value * value, axis=1, keepdims=True)


def both(value):
    half = value.shape[0] // 2
    total = value[:half] + value[half:]
    return jnp.concatenate([total, total], axis=0)


def tail(*columns):
    lane = lax.broadcasted_iota(jnp.int32, (columns[0].shape[0], LANES), 1)
    out = jnp.zeros(lane.shape, f32)
    for at, column in enumerate(columns):
        out = jnp.where(lane == at, column, out)
    return out


def apply_down(x_ref, first_ref, second_ref, turned, shots=slice(None)):
    stage(x_ref, first_ref, second_ref, -1)
    first, second = first_ref[...], second_ref[...]
    count = first.shape[0] // 2
    blocks = []
    for high, low in turned:
        total = dot(first, high[0, shots, :]) + dot(second, high[1, shots, :])
        rest = dot(first[:count], low[0, shots, :]) + dot(second[:count], low[1, shots, :])
        blocks.append(total[:count] + total[count:] + rest)
    return jnp.concatenate(blocks, axis=1)


def side(bits):
    me = lax.axis_index("rcv")
    first, second = ((me >> bit) & 1 for bit in bits)
    return first + (me & 1) * (second - first)


def project(value_ref, first_ref, second_ref, plain, extra, keep_ref, give_ref, bits):
    stage(value_ref, first_ref, second_ref, 1)
    rows = plain[0][0].shape[1]
    shots = plain[0][0].shape[2]
    half = value_ref.shape[0] // 2
    upper = side(bits) == 1
    for start in range(0, shots, shots // 2):
        columns = slice(start, start + shots // 2)
        total = 0.0
        for block, (high, low) in enumerate(plain):
            own = slice(block * rows, (block + 1) * rows)
            total = total + times(first_ref[:, own], second_ref[:, own], high, low, columns)
        keep_ref[:, columns] = jnp.where(upper, total[half:], total[:half])
        give_ref[:, columns] = jnp.where(upper, total[:half], total[half:])
    keep_ref[:, shots:] = jnp.where(upper, extra[half:], extra[:half])
    give_ref[:, shots:] = jnp.where(upper, extra[:half], extra[half:])


def collect(pieces, x_ref, ends_ref, bits):
    upper = side(bits)
    shots = x_ref.shape[1]
    for which, piece in enumerate(pieces):
        half = piece.shape[0]
        place = pl.ds(pl.multiple_of((upper ^ which) * half, half), half)
        x_ref[place, :] = piece[:, :shots]
        ends_ref[place, :] = piece[:, shots:]


def pairs(refs):
    return tuple((refs[at], refs[at + 1]) for at in range(0, len(refs), 2))


def rhs_kernel(bits, masks, *refs):
    sources, refs = refs[: len(masks)], refs[len(masks) :]
    down, refs = refs[:8], refs[8:]
    (ea, eb), (rhs_ref, *outs), (x_ref, f0, s0, f1, s1, *spread) = refs[:2], refs[2:5], refs[5:]
    half = x_ref.shape[0] // 2
    own = sources[0].shape[1]
    chip = lax.axis_index("rcv") >> 1
    for mask, source in zip(masks, sources):
        for part, value in enumerate((source[0], -source[1])):
            if spread:
                spread[0][part * half // own + (chip ^ mask)] = value
            else:
                x_ref[pl.ds(pl.multiple_of(part * half + (chip ^ mask) * own, own), own), :] = value
    for at in range(2 * half // own if spread else 0):
        x_ref[at * own : (at + 1) * own, :] = spread[0][at]
    rhs_ref[...] = apply_down(x_ref, f0, s0, pairs(down[4:]))
    energy = jnp.full((2 * half, 1), jnp.sum(ea[...] + eb[...]), f32)
    extra = tail(row_squares(rhs_ref[...]), energy)
    project(rhs_ref, f1, s1, pairs(down[:4]), extra, *outs, bits)


def first_kernel(bits, receivers, *refs):
    pieces, rhs_ref, down, refs = refs[:2], refs[2], refs[3:11], refs[11:]
    (x_ref, scalar_ref, image_ref, residual_ref, *outs), (ends_ref, f0, s0, f1, s1) = refs[:6], refs[6:]
    collect(pieces, x_ref, ends_ref, bits)
    norm = both(ends_ref[:, 0:1])
    damping = damping_ratio * ends_ref[:, 1:2] / receivers
    image = apply_down(x_ref, f0, s0, pairs(down[4:])) + damping * rhs_ref[...]
    image_ref[...] = image
    alpha = norm / (both(row_squares(x_ref[...])) + damping * norm)
    residual = rhs_ref[...] - alpha * image
    residual_ref[...] = residual
    scalar_ref[...] = tail(norm, damping, alpha)
    project(residual_ref, f1, s1, pairs(down[:4]), tail(row_squares(residual)), *outs, bits)


def last_kernel(bits, *refs):
    pieces, (rhs_ref, before_ref, scalar_ref, image_ref, residual_ref), turned = refs[:2], refs[2:7], refs[7:11]
    keep_ref, give_ref, x_ref, ends_ref, *scratch = refs[11:]
    collect(pieces, x_ref, ends_ref, bits)
    following = both(ends_ref[:, 0:1])
    norm = scalar_ref[:, 0:1]
    damping = scalar_ref[:, 1:2]
    alpha = scalar_ref[:, 2:3]
    beta = following / norm
    residual = residual_ref[...]
    image = apply_down(x_ref, *scratch, pairs(turned)) + beta * image_ref[...] + damping * residual
    curvature = both(row_squares(x_ref[...] + beta * before_ref[...])) + damping * (following + beta * following)
    alpha_next = following / curvature
    rhs = rhs_ref[...]
    found = alpha * rhs + alpha_next * (residual + beta * rhs)
    left = residual - alpha_next * image
    rows = turned[0].shape[2]
    keep_ref[0] = found[:, :rows]
    keep_ref[1] = left[:, :rows]
    give_ref[0] = found[:, rows:]
    give_ref[1] = left[:, rows:]


def order_kernel(own, *refs):
    pieces, (*outs, x_ref) = refs[: 2 * GROUPS], refs[2 * GROUPS :]
    upper = (lax.axis_index("rcv") & 1) == 1
    chips = pieces[0].shape[1] // (2 * own)
    for which, out_ref in enumerate(outs):
        for part in range(2):
            for chip in range(chips):
                source = pl.ds((part * chips + chip) * own, own)
                for group in range(GROUPS):
                    mine = pieces[2 * group][which, source, :]
                    other = pieces[2 * group + 1][which, source, :]
                    base = (2 * chip * GROUPS + group) * own
                    x_ref[base : base + own, :] = jnp.where(upper, other, mine)
                    base += GROUPS * own
                    x_ref[base : base + own, :] = jnp.where(upper, mine, other)
            out_ref[part] = x_ref[...].T


def body(down_spectra, up_sources, *, count, receivers):
    chip_bits = list(range(1, count.bit_length() - 1))
    orders = (chip_bits, chip_bits[::-1])
    ends = (chip_bits[0], chip_bits[-1])
    rows, shots = down_spectra.shape[1:]
    own = up_sources.shape[1] // GROUPS
    chips = count // 2
    packed = 2 * chips * own

    def swap(value, bit):
        return lax.ppermute(value, "rcv", [(at, at ^ (1 << bit)) for at in range(count)])

    def jump(value, mask):
        return lax.ppermute(value, "rcv", [(at, at ^ (mask << 1)) for at in range(count)])

    def turn(value, step):
        return lax.ppermute(value, "rcv", [(at, at ^ (1 << orders[at & 1][step])) for at in range(count)])

    def exchange(keep, give):
        keep = keep + turn(give, 0)
        for step in range(1, len(chip_bits)):
            keep = keep + turn(keep, step)
        return keep, turn(keep, 0)

    other_down = swap(down_spectra, 0)
    masks = sorted(range(chips), key=lambda mask: mask.bit_count())
    sources = []
    for group in range(GROUPS):
        part = up_sources[:, group * own : (group + 1) * own]
        sources.append([jump(part, mask) if mask else part for mask in masks])
    plain_a, turned_a, energy_a = split(pltpu.with_memory_space_constraint(down_spectra, pltpu.HBM))
    plain_b, turned_b, energy_b = split(other_down)
    turned = (*turned_a, *turned_b)
    down = (*plain_a, *plain_b, *turned)

    wide = [((2 * packed, shots), bf16)] * 2
    short = [((2 * packed, 2 * rows), bf16)] * 2
    lines = ((packed, 2 * rows), f32)
    every = ((packed, shots), f32)
    small = ((packed, LANES), f32)
    sent = [((packed // 2, shots + LANES), f32)] * 2
    spread = [((packed // own, own, shots), f32)] if own % 8 else []
    work = 2 * 2 * (3 * packed) * 2 * rows * shots

    state, sums = [], []
    for source in sources:
        rhs, *pair = call(
            functools.partial(rhs_kernel, ends, masks),
            [lines] + sent,
            (*source, *down, energy_a, energy_b),
            [every] + wide + short + spread,
            2 * work,
        )
        state.append((rhs,))
        sums.append(exchange(*pair))
    for group, (pieces, (rhs,)) in enumerate(zip(sums, state)):
        x, scalars, image, residual, *pair = call(
            functools.partial(first_kernel, ends, receivers),
            [every, small, lines, lines] + sent,
            (*pieces, rhs, *down),
            [small] + wide + short,
            2 * work,
        )
        state[group] = (rhs, x, scalars, image, residual)
        sums[group] = exchange(*pair)
    results = []
    for pieces, kept in zip(sums, state):
        keep, give = call(
            functools.partial(last_kernel, ends),
            [((2, packed, rows), f32)] * 2,
            (*pieces, *kept, *turned),
            [every, small] + wide,
            work,
        )
        results.append((keep, swap(give, 0)))

    pieces = [piece for pair in results for piece in pair]
    columns = GROUPS * packed
    return tuple(call(functools.partial(order_kernel, own), [((2, rows, columns), f32)] * 2, pieces, [((columns, rows), f32)]))


def solution(mesh):
    count = mesh.shape["rcv"]

    def run(down_spectra, up_sources):
        return body(down_spectra, up_sources, count=count, receivers=down_spectra.shape[1] * count)

    specs = (P("cuts", "rcv", None), P("cuts", "rcv", None))
    return jax.shard_map(run, mesh=mesh, in_specs=specs, out_specs=specs, check_vma=False)
```

```python
import functools
import jax
import jax.numpy as jnp
from jax import lax
from jax.experimental import pallas as pl
from jax.experimental.pallas import tpu as pltpu
from jax.sharding import PartitionSpec as P

damping_ratio = 0.1
LANES = 128
GROUPS = 2
ORDER = {'bE': ['a1.2']}
COST = {'bC.': 0.3, 'aL.': 0, 'aR': 30, 'bM': 10, 'bL.': 0, 'bC': 0, 'aC': 0.3, 'aC.': 3, 'aL': 0}
f32 = jnp.float32
bf16 = jnp.bfloat16


def dot(left, right):
    return lax.dot_general(left, right, (((1,), (0,)), ((), ())), preferred_element_type=f32)


def parts_of(value):
    high = value.astype(bf16)
    return high, (value - high.astype(f32)).astype(bf16)


def call(kernel, outs, args, scratch=(), flops=0, grid=(), in_specs=None):
    spec = pl.BlockSpec(memory_space=pltpu.VMEM)
    moved = sum(value.size * value.dtype.itemsize for value in args)
    return pl.pallas_call(
        kernel,
        out_shape=[jax.ShapeDtypeStruct(shape, dtype) for shape, dtype in outs],
        grid=grid,
        in_specs=in_specs or [spec] * len(args),
        out_specs=[spec] * len(outs),
        scratch_shapes=[pltpu.VMEM(shape, dtype) for shape, dtype in scratch],
        cost_estimate=pl.CostEstimate(flops=flops, transcendentals=0, bytes_accessed=moved),
        compiler_params=pltpu.CompilerParams(vmem_limit_bytes=16 << 20),
    )(*args)


def split_kernel(real_ref, imag_ref, high_ref, low_ref, turned_high_ref, turned_low_ref, energy_ref):
    rows, shots = real_ref.shape[1:]
    step, chunk = pl.program_id(0), pl.program_id(1)
    width = 2 * LANES
    at = slice(None) if rows == high_ref.shape[1] else pl.ds(pl.multiple_of(step * rows, rows), rows)

    @pl.when((step == 0) & (chunk == 0))
    def _():
        energy_ref[...] = jnp.zeros_like(energy_ref)

    for part, ref in enumerate((real_ref, imag_ref)):
        for start in range(0, shots, width):
            value = ref[0, :, start : start + width]
            place = pl.ds(pl.multiple_of(chunk * shots + start, width), width)
            high, low = parts_of(value)
            high_ref[part, at, place] = high
            low_ref[part, at, place] = low
            turned_high_ref[part, place, at] = high.T
            turned_low_ref[part, place, at] = low.T
            square = jnp.sum((value * value).reshape(rows // 8, 8, width), axis=0)
            energy_ref[...] += sum(square[:, lane : lane + LANES] for lane in range(0, width, LANES))


def split(value):
    _, rows, shots = value.shape
    block, chunks = min(rows, LANES), 2
    plain, turned = ((2, rows, shots), bf16), ((2, shots, rows), bf16)
    high, low, turned_high, turned_low, energy = call(
        split_kernel,
        [plain, plain, turned, turned, ((8, LANES), f32)],
        (value, value),
        grid=(rows // block, chunks),
        in_specs=[
            pl.BlockSpec((1, block, shots // chunks), lambda step, chunk: (0, step, chunk)),
            pl.BlockSpec((1, block, shots // chunks), lambda step, chunk: (1, step, chunk)),
        ],
    )
    return (high, low), (turned_high, turned_low), energy


def stage(value_ref, first_ref, second_ref, sign):
    half = value_ref.shape[0] // 2
    real = value_ref[:half, :]
    imag = value_ref[half:, :]
    for at, (a, b) in enumerate(zip(parts_of(real), parts_of(imag))):
        base = 2 * half * at
        first_ref[base : base + half, :] = a
        first_ref[base + half : base + 2 * half, :] = b
        second_ref[base : base + half, :] = b if sign > 0 else -b
        second_ref[base + half : base + 2 * half, :] = a if sign < 0 else -a


def times(first, second, high_ref, low_ref, columns=slice(None)):
    count = first.shape[0] // 2
    total = dot(first, high_ref[0, :, columns]) + dot(second, high_ref[1, :, columns])
    low = dot(first[:count], low_ref[0, :, columns]) + dot(second[:count], low_ref[1, :, columns])
    return total[:count] + total[count:] + low


def row_squares(value):
    return jnp.sum(value * value, axis=1, keepdims=True)


def both(value):
    half = value.shape[0] // 2
    total = value[:half] + value[half:]
    return jnp.concatenate([total, total], axis=0)


def tail(*columns):
    lane = lax.broadcasted_iota(jnp.int32, (columns[0].shape[0], LANES), 1)
    out = jnp.zeros(lane.shape, f32)
    for at, column in enumerate(columns):
        out = jnp.where(lane == at, column, out)
    return out


def apply_down(x_ref, first_ref, second_ref, turned, shots=slice(None)):
    stage(x_ref, first_ref, second_ref, -1)
    first, second = first_ref[...], second_ref[...]
    count = first.shape[0] // 2
    blocks = []
    for high, low in turned:
        total = dot(first, high[0, shots, :]) + dot(second, high[1, shots, :])
        rest = dot(first[:count], low[0, shots, :]) + dot(second[:count], low[1, shots, :])
        blocks.append(total[:count] + total[count:] + rest)
    return jnp.concatenate(blocks, axis=1)


def device_bit(bit):
    return (lax.axis_index("rcv") >> bit) & 1


def project(value_ref, first_ref, second_ref, plain, columns, keep_ref, give_ref, bit, extra=None):
    stage(value_ref, first_ref, second_ref, 1)
    rows = plain[0][0].shape[1]
    half = value_ref.shape[0] // 2
    front = columns.stop - columns.start
    total = 0.0
    for block, (high, low) in enumerate(plain):
        own = slice(block * rows, (block + 1) * rows)
        total = total + times(first_ref[:, own], second_ref[:, own], high, low, columns)
    upper = device_bit(bit) == 1
    keep_ref[:, :front] = jnp.where(upper, total[half:], total[:half])
    give_ref[:, :front] = jnp.where(upper, total[:half], total[half:])
    if extra is not None:
        keep_ref[:, front:] = jnp.where(upper, extra[half:], extra[:half])
        give_ref[:, front:] = jnp.where(upper, extra[:half], extra[half:])


def collect(pieces, x_ref, bit, ends_ref=None):
    upper = device_bit(bit)
    front = x_ref.shape[1]
    for which, piece in enumerate(pieces):
        half = piece.shape[0]
        place = pl.ds(pl.multiple_of((upper ^ which) * half, half), half)
        x_ref[place, :] = piece[:, :front]
        if ends_ref is not None:
            ends_ref[place, :] = piece[:, front:]


def pairs(refs):
    return tuple((refs[at], refs[at + 1]) for at in range(0, len(refs), 2))


def rhs_kernel(bit, masks, *refs):
    sources, refs = refs[: len(masks)], refs[len(masks) :]
    down, refs = refs[:8], refs[8:]
    (ea, eb), (rhs_ref, *outs), (x_ref, f0, s0, f1, s1, *spread) = refs[:2], refs[2:5], refs[5:]
    half = x_ref.shape[0] // 2
    own = sources[0].shape[1]
    chip = lax.axis_index("rcv") >> 1
    for mask, source in zip(masks, sources):
        for part, value in enumerate((source[0], -source[1])):
            if spread:
                spread[0][part * half // own + (chip ^ mask)] = value
            else:
                x_ref[pl.ds(pl.multiple_of(part * half + (chip ^ mask) * own, own), own), :] = value
    for at in range(2 * half // own if spread else 0):
        x_ref[at * own : (at + 1) * own, :] = spread[0][at]
    rhs_ref[...] = apply_down(x_ref, f0, s0, pairs(down[4:]))
    energy = jnp.full((2 * half, 1), jnp.sum(ea[...] + eb[...]), f32)
    extra = tail(row_squares(rhs_ref[...]), energy)
    front = outs[0].shape[1] - LANES
    project(rhs_ref, f1, s1, pairs(down[:4]), slice(0, front), *outs, bit, extra)


def back_kernel(bit, *refs):
    value_ref, down, outs, scratch = refs[0], refs[1:5], refs[5:7], refs[7:]
    shots = down[0].shape[2]
    project(value_ref, *scratch, pairs(down), slice(shots - outs[0].shape[1], shots), *outs, bit)


def front_kernel(bit, *refs):
    pieces, turned, (x_ref, ends_ref, image_ref), scratch = refs[:2], refs[2:6], refs[6:9], refs[9:]
    collect(pieces, x_ref, bit, ends_ref)
    image_ref[...] = apply_down(x_ref, *scratch, pairs(turned), slice(0, x_ref.shape[1]))


def first_kernel(bits, receivers, *refs):
    pieces, (before_ref, ends_ref, part_ref, rhs_ref, *refs) = refs[:2], refs[2:]
    down, refs = refs[:8], refs[8:]
    (x_ref, scalar_ref, image_ref, residual_ref, *outs), (f0, s0, f1, s1) = refs[:6], refs[6:]
    front = before_ref.shape[1]
    collect(pieces, x_ref, bits[1])
    norm = both(ends_ref[:, 0:1])
    damping = damping_ratio * ends_ref[:, 1:2] / receivers
    image = part_ref[...] + apply_down(x_ref, f0, s0, pairs(down[4:]), slice(front, None)) + damping * rhs_ref[...]
    image_ref[...] = image
    alpha = norm / (both(row_squares(before_ref[...]) + row_squares(x_ref[...])) + damping * norm)
    residual = rhs_ref[...] - alpha * image
    residual_ref[...] = residual
    scalar_ref[...] = tail(norm, damping, alpha)
    project(residual_ref, f1, s1, pairs(down[:4]), slice(0, front), *outs, bits[0], tail(row_squares(residual)))


def last_kernel(bit, *refs):
    pieces, (a_ref, ends_ref, part_ref, rhs_ref, before_a, before_b, scalar_ref, image_ref, residual_ref) = refs[:2], refs[2:11]
    turned, (keep_ref, give_ref, x_ref, *scratch) = refs[11:15], refs[15:]
    front = a_ref.shape[1]
    collect(pieces, x_ref, bit)
    following = both(ends_ref[:, 0:1])
    norm = scalar_ref[:, 0:1]
    damping = scalar_ref[:, 1:2]
    alpha = scalar_ref[:, 2:3]
    beta = following / norm
    residual = residual_ref[...]
    image = part_ref[...] + apply_down(x_ref, *scratch, pairs(turned), slice(front, None))
    image = image + beta * image_ref[...] + damping * residual
    squares = row_squares(a_ref[...] + beta * before_a[...]) + row_squares(x_ref[...] + beta * before_b[...])
    curvature = both(squares) + damping * (following + beta * following)
    alpha_next = following / curvature
    rhs = rhs_ref[...]
    found = alpha * rhs + alpha_next * (residual + beta * rhs)
    left = residual - alpha_next * image
    rows = turned[0].shape[2]
    keep_ref[0] = found[:, :rows]
    keep_ref[1] = left[:, :rows]
    give_ref[0] = found[:, rows:]
    give_ref[1] = left[:, rows:]


def order_kernel(own, *refs):
    pieces, (*outs, x_ref) = refs[: 2 * GROUPS], refs[2 * GROUPS :]
    upper = device_bit(0) == 1
    chips = pieces[0].shape[1] // (2 * own)
    for which, out_ref in enumerate(outs):
        for part in range(2):
            for chip in range(chips):
                source = pl.ds((part * chips + chip) * own, own)
                for group in range(GROUPS):
                    mine = pieces[2 * group][which, source, :]
                    other = pieces[2 * group + 1][which, source, :]
                    base = (2 * chip * GROUPS + group) * own
                    x_ref[base : base + own, :] = jnp.where(upper, other, mine)
                    base += GROUPS * own
                    x_ref[base : base + own, :] = jnp.where(upper, mine, other)
            out_ref[part] = x_ref[...].T


class Sum:
    def __init__(self, swap, order, pair):
        self.swap, self.order, self.at = swap, order, 0
        self.keep, give = pair
        self.other = swap(give, order[0])

    def step(self):
        self.at += 1
        self.keep = self.keep + self.other
        self.other = self.swap(self.keep, self.order[self.at % len(self.order)])


def body(down_spectra, up_sources, *, count, receivers):
    chip_bits = list(range(1, count.bit_length() - 1))
    orders = (chip_bits, chip_bits[::-1])
    ends = (chip_bits[0], chip_bits[-1])
    rows, shots = down_spectra.shape[1:]
    own = up_sources.shape[1] // GROUPS
    chips = count // 2
    packed = 2 * chips * own
    front = shots // 2

    def swap(value, bit):
        return lax.ppermute(value, "rcv", [(at, at ^ (1 << bit)) for at in range(count)])

    def jump(value, mask):
        return lax.ppermute(value, "rcv", [(at, at ^ (mask << 1)) for at in range(count)])

    other_down = swap(down_spectra, 0)
    masks = sorted(range(chips), key=lambda mask: mask.bit_count())
    sources = []
    for group in range(GROUPS):
        part = up_sources[:, group * own : (group + 1) * own]
        sources.append([jump(part, mask) if mask else part for mask in masks])
    plain_a, turned_a, energy_a = split(pltpu.with_memory_space_constraint(down_spectra, pltpu.HBM))
    plain_b, turned_b, energy_b = split(other_down)
    turned = (*turned_a, *turned_b)
    down = (*plain_a, *plain_b, *turned)

    wide = [((2 * packed, shots), bf16)] * 2
    narrow = [((2 * packed, front), bf16)] * 2
    short = [((2 * packed, 2 * rows), bf16)] * 2
    lines = ((packed, 2 * rows), f32)
    every = ((packed, shots), f32)
    ranged = ((packed, front), f32)
    small = ((packed, LANES), f32)
    work = 2 * 2 * 2 * (3 * packed) * rows * shots
    sent_0 = [((packed // 2, front + LANES), f32)] * 2
    sent_1 = [((packed // 2, front), f32)] * 2
    spread = [((packed // own, own, shots), f32)] if own % 8 else []
    plain = (*plain_a, *plain_b)

    done = {}

    def after(name, *values):
        for earlier in ORDER.get(name, ()):
            values = lax.optimization_barrier((done[earlier], *values))[1:]
        return values

    def launch(name, kernel, outs, args, scratch, flops):
        first, *rest = args
        results = call(kernel, outs, (*after(name, first), *rest), scratch, int(flops * COST.get(name, 1)))
        done[name] = results[0]
        return results

    def step(name, total):
        (total.keep,) = after(name, total.keep)
        total.step()
        done[name] = total.keep

    def way(name, which):
        return which ^ (name[0] == "b")

    def start(name, which, pair):
        return Sum(swap, orders[way(name, which)], pair)

    def back(name, value):
        kernel = functools.partial(back_kernel, ends[way(name, 1)])
        return start(name, 1, launch(name, kernel, sent_1, (value, *plain), short, work))

    def lead(name, total):
        kernel, pieces = functools.partial(front_kernel, ends[way(name, 0)]), (total.keep, total.other)
        return launch(name, kernel, [ranged, small, lines], (*pieces, *turned), narrow, work)

    def open_group(name, source):
        rhs, *pair = launch(
            name,
            functools.partial(rhs_kernel, ends[way(name, 0)], masks),
            [lines] + sent_0,
            (*source, *down, energy_a, energy_b),
            [every] + wide + short + spread,
            3 * work,
        )
        return rhs, start(name, 0, pair)

    def middle(name, total, led, rhs):
        before, norms, part = led
        x, scalars, image, residual, *pair = launch(
            name,
            functools.partial(first_kernel, (ends[way(name, 0)], ends[way(name, 1)]), receivers),
            [ranged, small, lines, lines] + sent_0,
            (total.keep, total.other, before, norms, part, rhs, *down),
            narrow + short,
            2 * work,
        )
        return (rhs, before, x, scalars, image, residual), start(name, 0, pair)

    def close(name, total, led, kept):
        keep, give = launch(
            name,
            functools.partial(last_kernel, ends[way(name, 1)]),
            [((2, packed, rows), f32)] * 2,
            (total.keep, total.other, *led, *kept, *turned),
            [ranged] + narrow,
            work,
        )
        return keep, swap(give, 0)

    def rounds(tag, a0, a1, b0, pending):
        step("a0" + tag, a0)
        step("a1" + tag, a1)
        b1 = back("bC" + tag, pending)
        for turn in range(2, len(chip_bits) + 1):
            end = tag + str(turn)
            step("a0" + end, a0)
            step("b0" + end, b0)
            step("b1" + end, b1)
            step("a1" + end, a1)
        led = lead("aL" + tag, a0)
        step("b0" + tag, b0)
        step("b1" + tag, b1)
        return b1, led

    rhs_a, a0 = open_group("aR", sources[0])
    a1 = back("aC", rhs_a)
    rhs_b, b0 = open_group("bR", sources[1])
    b1, led = rounds("", a0, a1, b0, rhs_b)
    kept_a, a0 = middle("aM", a1, led, rhs_a)
    a1 = back("aC.", kept_a[-1])
    led = lead("bL", b0)
    kept_b, b0 = middle("bM", b1, led, rhs_b)
    b1, led = rounds(".", a0, a1, b0, kept_b[-1])
    results = [close("aE", a1, led, kept_a)]
    led = lead("bL.", b0)
    results.append(close("bE", b1, led, kept_b))

    pieces = [piece for pair in results for piece in pair]
    columns = GROUPS * packed
    return tuple(call(functools.partial(order_kernel, own), [((2, rows, columns), f32)] * 2, pieces, [((columns, rows), f32)]))


def solution(mesh):
    count = mesh.shape["rcv"]

    def run(down_spectra, up_sources):
        return body(down_spectra, up_sources, count=count, receivers=down_spectra.shape[1] * count)

    specs = (P("cuts", "rcv", None), P("cuts", "rcv", None))
    return jax.shard_map(run, mesh=mesh, in_specs=specs, out_specs=specs, check_vma=False)
```

```python
import functools
import jax
import jax.numpy as jnp
from jax import lax
from jax.experimental import pallas as pl
from jax.experimental.pallas import tpu as pltpu
from jax.sharding import PartitionSpec as P

damping_ratio = 0.1
LANES = 128
GROUPS = 2
ORDER = {'bE': ['a1.2']}
COST = {'bC.': 0.3, 'aL.': 0, 'aR': 30, 'bM': 10, 'bL.': 0, 'bC': 0, 'aC': 0.3, 'aC.': 3, 'aL': 0}
f32 = jnp.float32
bf16 = jnp.bfloat16


def dot(left, right):
    return lax.dot_general(left, right, (((1,), (0,)), ((), ())), preferred_element_type=f32)


def parts_of(value):
    high = value.astype(bf16)
    return high, (value - high.astype(f32)).astype(bf16)


def call(kernel, outs, args, scratch=(), flops=0, grid=(), in_specs=None):
    spec = pl.BlockSpec(memory_space=pltpu.VMEM)
    moved = sum(value.size * value.dtype.itemsize for value in args)
    return pl.pallas_call(
        kernel,
        out_shape=[jax.ShapeDtypeStruct(shape, dtype) for shape, dtype in outs],
        grid=grid,
        in_specs=in_specs or [spec] * len(args),
        out_specs=[spec] * len(outs),
        scratch_shapes=[pltpu.VMEM(*item) if isinstance(item, tuple) else item for item in scratch],
        cost_estimate=pl.CostEstimate(flops=flops, transcendentals=0, bytes_accessed=moved),
        compiler_params=pltpu.CompilerParams(vmem_limit_bytes=16 << 20),
    )(*args)


def split_piece(value_of, part, at, places, high_ref, low_ref, turned_high_ref, turned_low_ref, energy_ref):
    for source, place in places:
        value = value_of(source)
        rows, width = value.shape
        high, low = parts_of(value)
        high_ref[part, at, place] = high
        low_ref[part, at, place] = low
        turned_high_ref[part, place, at] = high.T
        turned_low_ref[part, place, at] = low.T
        square = jnp.sum((value * value).reshape(rows // 8, 8, width), axis=0)
        energy_ref[...] += sum(square[:, lane : lane + LANES] for lane in range(0, width, LANES))


def split_kernel(real_ref, imag_ref, *outs):
    rows, shots = real_ref.shape[1:]
    step, chunk = pl.program_id(0), pl.program_id(1)
    width = 2 * LANES
    at = slice(None) if rows == outs[0].shape[1] else pl.ds(pl.multiple_of(step * rows, rows), rows)

    @pl.when((step == 0) & (chunk == 0))
    def _():
        outs[4][...] = jnp.zeros_like(outs[4])

    starts = range(0, shots, width)
    places = [
        (slice(start, start + width), pl.ds(pl.multiple_of(chunk * shots + start, width), width)) for start in starts
    ]
    for part, ref in enumerate((real_ref, imag_ref)):
        split_piece(lambda place: ref[0, :, place], part, at, places, *outs)


def fetch_split_kernel(down_ref, *refs):
    outs, (held_ref, sems) = refs[:5], refs[5:]
    rows, shots = down_ref.shape[1:]
    block, chunks, width = min(rows, LANES), 2, 2 * LANES
    pieces = []
    for part in range(2):
        for row in range(0, rows, block):
            for chunk in range(chunks):
                start = chunk * shots // chunks
                where = (part, slice(row, row + block), slice(start, start + shots // chunks))
                copy = pltpu.make_async_copy(down_ref.at[where], held_ref.at[where], sems.at[len(pieces)])
                copy.start()
                pieces.append((copy, where))
    outs[4][...] = jnp.zeros_like(outs[4])
    for copy, (part, at, where) in pieces:
        copy.wait()
        places = [(slice(start, start + width),) * 2 for start in range(where.start, where.stop, width)]
        split_piece(lambda place: held_ref[part, at, place], part, at, places, *outs)


def split(value, from_hbm=False):
    _, rows, shots = value.shape
    block, chunks = min(rows, LANES), 2
    plain, turned = ((2, rows, shots), bf16), ((2, shots, rows), bf16)
    outs = [plain, plain, turned, turned, ((8, LANES), f32)]
    if from_hbm:
        pieces = 2 * (rows // block) * chunks
        high, low, turned_high, turned_low, energy = call(
            fetch_split_kernel,
            outs,
            (value,),
            [pltpu.VMEM(value.shape, f32), pltpu.SemaphoreType.DMA((pieces,))],
            in_specs=[pl.BlockSpec(memory_space=pltpu.HBM)],
        )
    else:
        high, low, turned_high, turned_low, energy = call(
            split_kernel,
            outs,
            (value, value),
            grid=(rows // block, chunks),
            in_specs=[
                pl.BlockSpec((1, block, shots // chunks), lambda step, chunk: (0, step, chunk)),
                pl.BlockSpec((1, block, shots // chunks), lambda step, chunk: (1, step, chunk)),
            ],
        )
    return (high, low), (turned_high, turned_low), energy


def stage(value_ref, first_ref, second_ref, sign):
    half = value_ref.shape[0] // 2
    real = value_ref[:half, :]
    imag = value_ref[half:, :]
    for at, (a, b) in enumerate(zip(parts_of(real), parts_of(imag))):
        base = 2 * half * at
        first_ref[base : base + half, :] = a
        first_ref[base + half : base + 2 * half, :] = b
        second_ref[base : base + half, :] = b if sign > 0 else -b
        second_ref[base + half : base + 2 * half, :] = a if sign < 0 else -a


def times(first, second, high_ref, low_ref, columns=slice(None)):
    count = first.shape[0] // 2
    total = dot(first, high_ref[0, :, columns]) + dot(second, high_ref[1, :, columns])
    low = dot(first[:count], low_ref[0, :, columns]) + dot(second[:count], low_ref[1, :, columns])
    return total[:count] + total[count:] + low


def row_squares(value):
    return jnp.sum(value * value, axis=1, keepdims=True)


def both(value):
    half = value.shape[0] // 2
    total = value[:half] + value[half:]
    return jnp.concatenate([total, total], axis=0)


def tail(*columns):
    lane = lax.broadcasted_iota(jnp.int32, (columns[0].shape[0], LANES), 1)
    out = jnp.zeros(lane.shape, f32)
    for at, column in enumerate(columns):
        out = jnp.where(lane == at, column, out)
    return out


def apply_down(x_ref, first_ref, second_ref, turned, shots=slice(None)):
    stage(x_ref, first_ref, second_ref, -1)
    first, second = first_ref[...], second_ref[...]
    count = first.shape[0] // 2
    blocks = []
    for high, low in turned:
        total = dot(first, high[0, shots, :]) + dot(second, high[1, shots, :])
        rest = dot(first[:count], low[0, shots, :]) + dot(second[:count], low[1, shots, :])
        blocks.append(total[:count] + total[count:] + rest)
    return jnp.concatenate(blocks, axis=1)


def device_bit(bit):
    return (lax.axis_index("rcv") >> bit) & 1


def project(value_ref, first_ref, second_ref, plain, columns, keep_ref, give_ref, bit, extra=None):
    stage(value_ref, first_ref, second_ref, 1)
    rows = plain[0][0].shape[1]
    half = value_ref.shape[0] // 2
    front = columns.stop - columns.start
    total = 0.0
    for block, (high, low) in enumerate(plain):
        own = slice(block * rows, (block + 1) * rows)
        total = total + times(first_ref[:, own], second_ref[:, own], high, low, columns)
    upper = device_bit(bit) == 1
    keep_ref[:, :front] = jnp.where(upper, total[half:], total[:half])
    give_ref[:, :front] = jnp.where(upper, total[:half], total[half:])
    if extra is not None:
        keep_ref[:, front:] = jnp.where(upper, extra[half:], extra[:half])
        give_ref[:, front:] = jnp.where(upper, extra[:half], extra[half:])


def collect(pieces, x_ref, bit, ends_ref=None):
    upper = device_bit(bit)
    front = x_ref.shape[1]
    for which, piece in enumerate(pieces):
        half = piece.shape[0]
        place = pl.ds(pl.multiple_of((upper ^ which) * half, half), half)
        x_ref[place, :] = piece[:, :front]
        if ends_ref is not None:
            ends_ref[place, :] = piece[:, front:]


def pairs(refs):
    return tuple((refs[at], refs[at + 1]) for at in range(0, len(refs), 2))


def rhs_kernel(bit, masks, *refs):
    sources, refs = refs[: len(masks)], refs[len(masks) :]
    down, refs = refs[:8], refs[8:]
    (ea, eb), (rhs_ref, *outs), (x_ref, f0, s0, f1, s1, *spread) = refs[:2], refs[2:5], refs[5:]
    half = x_ref.shape[0] // 2
    own = sources[0].shape[1]
    chip = lax.axis_index("rcv") >> 1
    for mask, source in zip(masks, sources):
        for part, value in enumerate((source[0], -source[1])):
            if spread:
                spread[0][part * half // own + (chip ^ mask)] = value
            else:
                x_ref[pl.ds(pl.multiple_of(part * half + (chip ^ mask) * own, own), own), :] = value
    for at in range(2 * half // own if spread else 0):
        x_ref[at * own : (at + 1) * own, :] = spread[0][at]
    rhs_ref[...] = apply_down(x_ref, f0, s0, pairs(down[4:]))
    energy = jnp.full((2 * half, 1), jnp.sum(ea[...] + eb[...]), f32)
    extra = tail(row_squares(rhs_ref[...]), energy)
    front = outs[0].shape[1] - LANES
    project(rhs_ref, f1, s1, pairs(down[:4]), slice(0, front), *outs, bit, extra)


def back_kernel(bit, *refs):
    value_ref, down, outs, scratch = refs[0], refs[1:5], refs[5:7], refs[7:]
    shots = down[0].shape[2]
    project(value_ref, *scratch, pairs(down), slice(shots - outs[0].shape[1], shots), *outs, bit)


def front_kernel(bit, *refs):
    pieces, turned, (x_ref, ends_ref, image_ref), scratch = refs[:2], refs[2:6], refs[6:9], refs[9:]
    collect(pieces, x_ref, bit, ends_ref)
    image_ref[...] = apply_down(x_ref, *scratch, pairs(turned), slice(0, x_ref.shape[1]))


def first_kernel(bits, receivers, *refs):
    pieces, (before_ref, ends_ref, part_ref, rhs_ref, *refs) = refs[:2], refs[2:]
    down, refs = refs[:8], refs[8:]
    (x_ref, scalar_ref, image_ref, residual_ref, *outs), (f0, s0, f1, s1) = refs[:6], refs[6:]
    front = before_ref.shape[1]
    collect(pieces, x_ref, bits[1])
    norm = both(ends_ref[:, 0:1])
    damping = damping_ratio * ends_ref[:, 1:2] / receivers
    image = part_ref[...] + apply_down(x_ref, f0, s0, pairs(down[4:]), slice(front, None)) + damping * rhs_ref[...]
    image_ref[...] = image
    alpha = norm / (both(row_squares(before_ref[...]) + row_squares(x_ref[...])) + damping * norm)
    residual = rhs_ref[...] - alpha * image
    residual_ref[...] = residual
    scalar_ref[...] = tail(norm, damping, alpha)
    project(residual_ref, f1, s1, pairs(down[:4]), slice(0, front), *outs, bits[0], tail(row_squares(residual)))


def last_kernel(bit, *refs):
    pieces, (a_ref, ends_ref, part_ref, rhs_ref, before_a, before_b, scalar_ref, image_ref, residual_ref) = refs[:2], refs[2:11]
    turned, (keep_ref, give_ref, x_ref, *scratch) = refs[11:15], refs[15:]
    front = a_ref.shape[1]
    collect(pieces, x_ref, bit)
    following = both(ends_ref[:, 0:1])
    norm = scalar_ref[:, 0:1]
    damping = scalar_ref[:, 1:2]
    alpha = scalar_ref[:, 2:3]
    beta = following / norm
    residual = residual_ref[...]
    image = part_ref[...] + apply_down(x_ref, *scratch, pairs(turned), slice(front, None))
    image = image + beta * image_ref[...] + damping * residual
    squares = row_squares(a_ref[...] + beta * before_a[...]) + row_squares(x_ref[...] + beta * before_b[...])
    curvature = both(squares) + damping * (following + beta * following)
    alpha_next = following / curvature
    rhs = rhs_ref[...]
    found = alpha * rhs + alpha_next * (residual + beta * rhs)
    left = residual - alpha_next * image
    rows = turned[0].shape[2]
    keep_ref[0] = found[:, :rows]
    keep_ref[1] = left[:, :rows]
    give_ref[0] = found[:, rows:]
    give_ref[1] = left[:, rows:]


def order_kernel(own, *refs):
    pieces, (*outs, x_ref) = refs[: 2 * GROUPS], refs[2 * GROUPS :]
    upper = device_bit(0) == 1
    chips = pieces[0].shape[1] // (2 * own)
    for which, out_ref in enumerate(outs):
        for part in range(2):
            for chip in range(chips):
                source = pl.ds((part * chips + chip) * own, own)
                for group in range(GROUPS):
                    mine = pieces[2 * group][which, source, :]
                    other = pieces[2 * group + 1][which, source, :]
                    base = (2 * chip * GROUPS + group) * own
                    x_ref[base : base + own, :] = jnp.where(upper, other, mine)
                    base += GROUPS * own
                    x_ref[base : base + own, :] = jnp.where(upper, mine, other)
            out_ref[part] = x_ref[...].T


class Sum:
    def __init__(self, swap, order, pair):
        self.swap, self.order, self.at = swap, order, 0
        self.keep, give = pair
        self.other = swap(give, order[0])

    def step(self):
        self.at += 1
        self.keep = self.keep + self.other
        self.other = self.swap(self.keep, self.order[self.at % len(self.order)])


def body(down_spectra, up_sources, *, count, receivers):
    chip_bits = list(range(1, count.bit_length() - 1))
    orders = (chip_bits, chip_bits[::-1])
    ends = (chip_bits[0], chip_bits[-1])
    rows, shots = down_spectra.shape[1:]
    own = up_sources.shape[1] // GROUPS
    chips = count // 2
    packed = 2 * chips * own
    front = shots // 2

    def swap(value, bit):
        return lax.ppermute(value, "rcv", [(at, at ^ (1 << bit)) for at in range(count)])

    def jump(value, mask):
        return lax.ppermute(value, "rcv", [(at, at ^ (mask << 1)) for at in range(count)])

    other_down = swap(down_spectra, 0)
    masks = sorted(range(chips), key=lambda mask: mask.bit_count())
    sources = []
    for group in range(GROUPS):
        part = up_sources[:, group * own : (group + 1) * own]
        sources.append([jump(part, mask) if mask else part for mask in masks])
    plain_a, turned_a, energy_a = split(down_spectra, from_hbm=True)
    plain_b, turned_b, energy_b = split(other_down)
    turned = (*turned_a, *turned_b)
    down = (*plain_a, *plain_b, *turned)

    wide = [((2 * packed, shots), bf16)] * 2
    narrow = [((2 * packed, front), bf16)] * 2
    short = [((2 * packed, 2 * rows), bf16)] * 2
    lines = ((packed, 2 * rows), f32)
    every = ((packed, shots), f32)
    ranged = ((packed, front), f32)
    small = ((packed, LANES), f32)
    work = 2 * 2 * 2 * (3 * packed) * rows * shots
    sent_0 = [((packed // 2, front + LANES), f32)] * 2
    sent_1 = [((packed // 2, front), f32)] * 2
    spread = [((packed // own, own, shots), f32)] if own % 8 else []
    plain = (*plain_a, *plain_b)

    done = {}

    def after(name, *values):
        for earlier in ORDER.get(name, ()):
            values = lax.optimization_barrier((done[earlier], *values))[1:]
        return values

    def launch(name, kernel, outs, args, scratch, flops):
        first, *rest = args
        results = call(kernel, outs, (*after(name, first), *rest), scratch, int(flops * COST.get(name, 1)))
        done[name] = results[0]
        return results

    def step(name, total):
        (total.keep,) = after(name, total.keep)
        total.step()
        done[name] = total.keep

    def way(name, which):
        return which ^ (name[0] == "b")

    def start(name, which, pair):
        return Sum(swap, orders[way(name, which)], pair)

    def back(name, value):
        kernel = functools.partial(back_kernel, ends[way(name, 1)])
        return start(name, 1, launch(name, kernel, sent_1, (value, *plain), short, work))

    def lead(name, total):
        kernel, pieces = functools.partial(front_kernel, ends[way(name, 0)]), (total.keep, total.other)
        return launch(name, kernel, [ranged, small, lines], (*pieces, *turned), narrow, work)

    def open_group(name, source):
        rhs, *pair = launch(
            name,
            functools.partial(rhs_kernel, ends[way(name, 0)], masks),
            [lines] + sent_0,
            (*source, *down, energy_a, energy_b),
            [every] + wide + short + spread,
            3 * work,
        )
        return rhs, start(name, 0, pair)

    def middle(name, total, led, rhs):
        before, norms, part = led
        x, scalars, image, residual, *pair = launch(
            name,
            functools.partial(first_kernel, (ends[way(name, 0)], ends[way(name, 1)]), receivers),
            [ranged, small, lines, lines] + sent_0,
            (total.keep, total.other, before, norms, part, rhs, *down),
            narrow + short,
            2 * work,
        )
        return (rhs, before, x, scalars, image, residual), start(name, 0, pair)

    def close(name, total, led, kept):
        keep, give = launch(
            name,
            functools.partial(last_kernel, ends[way(name, 1)]),
            [((2, packed, rows), f32)] * 2,
            (total.keep, total.other, *led, *kept, *turned),
            [ranged] + narrow,
            work,
        )
        return keep, swap(give, 0)

    def rounds(tag, a0, a1, b0, pending):
        step("a0" + tag, a0)
        step("a1" + tag, a1)
        b1 = back("bC" + tag, pending)
        for turn in range(2, len(chip_bits) + 1):
            end = tag + str(turn)
            step("a0" + end, a0)
            step("b0" + end, b0)
            step("b1" + end, b1)
            step("a1" + end, a1)
        led = lead("aL" + tag, a0)
        step("b0" + tag, b0)
        step("b1" + tag, b1)
        return b1, led

    rhs_a, a0 = open_group("aR", sources[0])
    a1 = back("aC", rhs_a)
    rhs_b, b0 = open_group("bR", sources[1])
    b1, led = rounds("", a0, a1, b0, rhs_b)
    kept_a, a0 = middle("aM", a1, led, rhs_a)
    a1 = back("aC.", kept_a[-1])
    led = lead("bL", b0)
    kept_b, b0 = middle("bM", b1, led, rhs_b)
    b1, led = rounds(".", a0, a1, b0, kept_b[-1])
    results = [close("aE", a1, led, kept_a)]
    led = lead("bL.", b0)
    results.append(close("bE", b1, led, kept_b))

    pieces = [piece for pair in results for piece in pair]
    columns = GROUPS * packed
    return tuple(call(functools.partial(order_kernel, own), [((2, rows, columns), f32)] * 2, pieces, [((columns, rows), f32)]))


def solution(mesh):
    count = mesh.shape["rcv"]

    def run(down_spectra, up_sources):
        return body(down_spectra, up_sources, count=count, receivers=down_spectra.shape[1] * count)

    specs = (P("cuts", "rcv", None), P("cuts", "rcv", None))
    return jax.shard_map(run, mesh=mesh, in_specs=specs, out_specs=specs, check_vma=False)
```

```python
import functools
import jax
import jax.numpy as jnp
from jax import lax
from jax.experimental import pallas as pl
from jax.experimental.pallas import tpu as pltpu
from jax.sharding import PartitionSpec as P

damping_ratio = 0.1
LANES = 128
GROUPS = 2
ORDER = {'bE': ['a1.2']}
COST = {'bC.': 0.3, 'aL.': 0, 'aR': 30, 'bM': 10, 'bL.': 0, 'bC': 0, 'aC': 0.3, 'aC.': 3, 'aL': 0}
f32 = jnp.float32
bf16 = jnp.bfloat16


def dot(left, right):
    return lax.dot_general(left, right, (((1,), (0,)), ((), ())), preferred_element_type=f32)


def parts_of(value):
    high = value.astype(bf16)
    return high, (value - high.astype(f32)).astype(bf16)


def call(kernel, outs, args, scratch=(), flops=0, in_specs=None):
    spec = pl.BlockSpec(memory_space=pltpu.VMEM)
    moved = sum(value.size * value.dtype.itemsize for value in args)
    return pl.pallas_call(
        kernel,
        out_shape=[jax.ShapeDtypeStruct(shape, dtype) for shape, dtype in outs],
        in_specs=in_specs or [spec] * len(args),
        out_specs=[spec] * len(outs),
        scratch_shapes=[pltpu.VMEM(*item) if isinstance(item, tuple) else item for item in scratch],
        cost_estimate=pl.CostEstimate(flops=flops, transcendentals=0, bytes_accessed=moved),
        compiler_params=pltpu.CompilerParams(vmem_limit_bytes=16 << 20),
    )(*args)


def split_piece(down_ref, part, at, places, high_ref, low_ref, turned_high_ref, turned_low_ref, energy_ref):
    for place in places:
        value = down_ref[part, at, place]
        rows, width = value.shape
        high, low = parts_of(value)
        high_ref[part, at, place] = high
        low_ref[part, at, place] = low
        turned_high_ref[part, place, at] = high.T
        turned_low_ref[part, place, at] = low.T
        square = jnp.sum((value * value).reshape(rows // 8, 8, width), axis=0)
        energy_ref[...] += sum(square[:, lane : lane + LANES] for lane in range(0, width, LANES))


def pieces_of(shape):
    _, rows, shots = shape
    block, width = min(rows, LANES), shots // 2
    starts = [(row, start) for row in range(0, rows, block) for start in range(0, shots, width)]
    return [(part, slice(row, row + block), slice(start, start + width)) for part in range(2) for row, start in starts]


def places_of(shots):
    width = 2 * LANES
    return [slice(start, start + width) for start in range(shots.start, shots.stop, width)]


def split_kernel(down_ref, *outs):
    outs[4][...] = jnp.zeros_like(outs[4])
    for part, at, shots in pieces_of(down_ref.shape):
        split_piece(down_ref, part, at, places_of(shots), *outs)


def fetch_split_kernel(down_ref, *refs):
    outs, (held_ref, sems) = refs[:5], refs[5:]
    copies = []
    for where in pieces_of(down_ref.shape):
        copies.append(pltpu.make_async_copy(down_ref.at[where], held_ref.at[where], sems.at[len(copies)]))
        copies[-1].start()
    outs[4][...] = jnp.zeros_like(outs[4])
    for copy, (part, at, shots) in zip(copies, pieces_of(down_ref.shape)):
        copy.wait()
        split_piece(held_ref, part, at, places_of(shots), *outs)


def split(value, from_hbm=False):
    _, rows, shots = value.shape
    plain, turned = ((2, rows, shots), bf16), ((2, shots, rows), bf16)
    outs = [plain, plain, turned, turned, ((8, LANES), f32)]
    if from_hbm:
        value = pltpu.with_memory_space_constraint(value, pltpu.HBM)
        scratch = [pltpu.VMEM(value.shape, f32), pltpu.SemaphoreType.DMA((len(pieces_of(value.shape)),))]
        specs = [pl.BlockSpec(memory_space=pltpu.HBM)]
        high, low, turned_high, turned_low, energy = call(fetch_split_kernel, outs, (value,), scratch, in_specs=specs)
    else:
        high, low, turned_high, turned_low, energy = call(split_kernel, outs, (value,))
    return (high, low), (turned_high, turned_low), energy


def stage(value_ref, first_ref, second_ref, sign):
    half = value_ref.shape[0] // 2
    real = value_ref[:half, :]
    imag = value_ref[half:, :]
    for at, (a, b) in enumerate(zip(parts_of(real), parts_of(imag))):
        base = 2 * half * at
        first_ref[base : base + half, :] = a
        first_ref[base + half : base + 2 * half, :] = b
        second_ref[base : base + half, :] = b if sign > 0 else -b
        second_ref[base + half : base + 2 * half, :] = a if sign < 0 else -a


def times(first, second, high_ref, low_ref, columns=slice(None)):
    count = first.shape[0] // 2
    total = dot(first, high_ref[0, :, columns]) + dot(second, high_ref[1, :, columns])
    low = dot(first[:count], low_ref[0, :, columns]) + dot(second[:count], low_ref[1, :, columns])
    return total[:count] + total[count:] + low


def row_squares(value):
    return jnp.sum(value * value, axis=1, keepdims=True)


def both(value):
    half = value.shape[0] // 2
    total = value[:half] + value[half:]
    return jnp.concatenate([total, total], axis=0)


def tail(*columns):
    lane = lax.broadcasted_iota(jnp.int32, (columns[0].shape[0], LANES), 1)
    out = jnp.zeros(lane.shape, f32)
    for at, column in enumerate(columns):
        out = jnp.where(lane == at, column, out)
    return out


def apply_down(x_ref, first_ref, second_ref, turned, shots=slice(None)):
    stage(x_ref, first_ref, second_ref, -1)
    first, second = first_ref[...], second_ref[...]
    count = first.shape[0] // 2
    blocks = []
    for high, low in turned:
        total = dot(first, high[0, shots, :]) + dot(second, high[1, shots, :])
        rest = dot(first[:count], low[0, shots, :]) + dot(second[:count], low[1, shots, :])
        blocks.append(total[:count] + total[count:] + rest)
    return jnp.concatenate(blocks, axis=1)


def device_bit(bit):
    return (lax.axis_index("rcv") >> bit) & 1


def project(value_ref, first_ref, second_ref, plain, columns, keep_ref, give_ref, bit, extra=None):
    stage(value_ref, first_ref, second_ref, 1)
    rows = plain[0][0].shape[1]
    half = value_ref.shape[0] // 2
    front = columns.stop - columns.start
    total = 0.0
    for block, (high, low) in enumerate(plain):
        own = slice(block * rows, (block + 1) * rows)
        total = total + times(first_ref[:, own], second_ref[:, own], high, low, columns)
    upper = device_bit(bit) == 1
    keep_ref[:, :front] = jnp.where(upper, total[half:], total[:half])
    give_ref[:, :front] = jnp.where(upper, total[:half], total[half:])
    if extra is not None:
        keep_ref[:, front:] = jnp.where(upper, extra[half:], extra[:half])
        give_ref[:, front:] = jnp.where(upper, extra[:half], extra[half:])


def collect(pieces, x_ref, bit, ends_ref=None):
    upper = device_bit(bit)
    front = x_ref.shape[1]
    for which, piece in enumerate(pieces):
        half = piece.shape[0]
        place = pl.ds(pl.multiple_of((upper ^ which) * half, half), half)
        x_ref[place, :] = piece[:, :front]
        if ends_ref is not None:
            ends_ref[place, :] = piece[:, front:]


def pairs(refs):
    return tuple((refs[at], refs[at + 1]) for at in range(0, len(refs), 2))


def rhs_kernel(bit, masks, *refs):
    sources, refs = refs[: len(masks)], refs[len(masks) :]
    down, refs = refs[:8], refs[8:]
    (ea, eb), (rhs_ref, *outs), (x_ref, f0, s0, f1, s1, *spread) = refs[:2], refs[2:5], refs[5:]
    half = x_ref.shape[0] // 2
    own = sources[0].shape[1]
    chip = lax.axis_index("rcv") >> 1
    for mask, source in zip(masks, sources):
        for part, value in enumerate((source[0], -source[1])):
            if spread:
                spread[0][part * half // own + (chip ^ mask)] = value
            else:
                x_ref[pl.ds(pl.multiple_of(part * half + (chip ^ mask) * own, own), own), :] = value
    for at in range(2 * half // own if spread else 0):
        x_ref[at * own : (at + 1) * own, :] = spread[0][at]
    rhs_ref[...] = apply_down(x_ref, f0, s0, pairs(down[4:]))
    energy = jnp.full((2 * half, 1), jnp.sum(ea[...] + eb[...]), f32)
    extra = tail(row_squares(rhs_ref[...]), energy)
    front = outs[0].shape[1] - LANES
    project(rhs_ref, f1, s1, pairs(down[:4]), slice(0, front), *outs, bit, extra)


def back_kernel(bit, *refs):
    value_ref, down, outs, scratch = refs[0], refs[1:5], refs[5:7], refs[7:]
    shots = down[0].shape[2]
    project(value_ref, *scratch, pairs(down), slice(shots - outs[0].shape[1], shots), *outs, bit)


def front_kernel(bit, *refs):
    pieces, turned, (x_ref, ends_ref, image_ref), scratch = refs[:2], refs[2:6], refs[6:9], refs[9:]
    collect(pieces, x_ref, bit, ends_ref)
    image_ref[...] = apply_down(x_ref, *scratch, pairs(turned), slice(0, x_ref.shape[1]))


def first_kernel(bits, receivers, *refs):
    pieces, (before_ref, ends_ref, part_ref, rhs_ref, *refs) = refs[:2], refs[2:]
    down, refs = refs[:8], refs[8:]
    (x_ref, scalar_ref, image_ref, residual_ref, *outs), (f0, s0, f1, s1) = refs[:6], refs[6:]
    front = before_ref.shape[1]
    collect(pieces, x_ref, bits[1])
    norm = both(ends_ref[:, 0:1])
    damping = damping_ratio * ends_ref[:, 1:2] / receivers
    image = part_ref[...] + apply_down(x_ref, f0, s0, pairs(down[4:]), slice(front, None)) + damping * rhs_ref[...]
    image_ref[...] = image
    alpha = norm / (both(row_squares(before_ref[...]) + row_squares(x_ref[...])) + damping * norm)
    residual = rhs_ref[...] - alpha * image
    residual_ref[...] = residual
    scalar_ref[...] = tail(norm, damping, alpha)
    project(residual_ref, f1, s1, pairs(down[:4]), slice(0, front), *outs, bits[0], tail(row_squares(residual)))


def last_kernel(bit, *refs):
    pieces, (a_ref, ends_ref, part_ref, rhs_ref, before_a, before_b, scalar_ref, image_ref, residual_ref) = refs[:2], refs[2:11]
    turned, (keep_ref, give_ref, x_ref, *scratch) = refs[11:15], refs[15:]
    front = a_ref.shape[1]
    collect(pieces, x_ref, bit)
    following = both(ends_ref[:, 0:1])
    norm = scalar_ref[:, 0:1]
    damping = scalar_ref[:, 1:2]
    alpha = scalar_ref[:, 2:3]
    beta = following / norm
    residual = residual_ref[...]
    image = part_ref[...] + apply_down(x_ref, *scratch, pairs(turned), slice(front, None))
    image = image + beta * image_ref[...] + damping * residual
    squares = row_squares(a_ref[...] + beta * before_a[...]) + row_squares(x_ref[...] + beta * before_b[...])
    curvature = both(squares) + damping * (following + beta * following)
    alpha_next = following / curvature
    rhs = rhs_ref[...]
    found = alpha * rhs + alpha_next * (residual + beta * rhs)
    left = residual - alpha_next * image
    rows = turned[0].shape[2]
    keep_ref[0] = found[:, :rows]
    keep_ref[1] = left[:, :rows]
    give_ref[0] = found[:, rows:]
    give_ref[1] = left[:, rows:]


def order_kernel(own, *refs):
    pieces, (*outs, x_ref) = refs[: 2 * GROUPS], refs[2 * GROUPS :]
    upper = device_bit(0) == 1
    chips = pieces[0].shape[1] // (2 * own)
    for which, out_ref in enumerate(outs):
        for part in range(2):
            for chip in range(chips):
                source = pl.ds((part * chips + chip) * own, own)
                for group in range(GROUPS):
                    mine = pieces[2 * group][which, source, :]
                    other = pieces[2 * group + 1][which, source, :]
                    base = (2 * chip * GROUPS + group) * own
                    x_ref[base : base + own, :] = jnp.where(upper, other, mine)
                    base += GROUPS * own
                    x_ref[base : base + own, :] = jnp.where(upper, mine, other)
            out_ref[part] = x_ref[...].T


class Sum:
    def __init__(self, swap, order, pair):
        self.swap, self.order, self.at = swap, order, 0
        self.keep, give = pair
        self.other = swap(give, order[0])

    def step(self):
        self.at += 1
        self.keep = self.keep + self.other
        self.other = self.swap(self.keep, self.order[self.at % len(self.order)])


def body(down_spectra, up_sources, *, count, receivers):
    chip_bits = list(range(1, count.bit_length() - 1))
    orders = (chip_bits, chip_bits[::-1])
    ends = (chip_bits[0], chip_bits[-1])
    rows, shots = down_spectra.shape[1:]
    own = up_sources.shape[1] // GROUPS
    chips = count // 2
    packed = 2 * chips * own
    front = shots // 2

    def swap(value, bit):
        return lax.ppermute(value, "rcv", [(at, at ^ (1 << bit)) for at in range(count)])

    def jump(value, mask):
        return lax.ppermute(value, "rcv", [(at, at ^ (mask << 1)) for at in range(count)])

    other_down = swap(down_spectra, 0)
    masks = sorted(range(chips), key=lambda mask: mask.bit_count())
    sources = []
    for group in range(GROUPS):
        part = up_sources[:, group * own : (group + 1) * own]
        sources.append([jump(part, mask) if mask else part for mask in masks])
    plain_a, turned_a, energy_a = split(down_spectra, from_hbm=True)
    plain_b, turned_b, energy_b = split(other_down)
    turned = (*turned_a, *turned_b)
    down = (*plain_a, *plain_b, *turned)

    wide = [((2 * packed, shots), bf16)] * 2
    narrow = [((2 * packed, front), bf16)] * 2
    short = [((2 * packed, 2 * rows), bf16)] * 2
    lines = ((packed, 2 * rows), f32)
    every = ((packed, shots), f32)
    ranged = ((packed, front), f32)
    small = ((packed, LANES), f32)
    work = 2 * 2 * 2 * (3 * packed) * rows * shots
    sent_0 = [((packed // 2, front + LANES), f32)] * 2
    sent_1 = [((packed // 2, front), f32)] * 2
    spread = [((packed // own, own, shots), f32)] if own % 8 else []
    plain = (*plain_a, *plain_b)

    done = {}

    def after(name, *values):
        for earlier in ORDER.get(name, ()):
            values = lax.optimization_barrier((done[earlier], *values))[1:]
        return values

    def launch(name, kernel, outs, args, scratch, flops):
        first, *rest = args
        results = call(kernel, outs, (*after(name, first), *rest), scratch, int(flops * COST.get(name, 1)))
        done[name] = results[0]
        return results

    def step(name, total):
        (total.keep,) = after(name, total.keep)
        total.step()
        done[name] = total.keep

    def way(name, which):
        return which ^ (name[0] == "b")

    def start(name, which, pair):
        return Sum(swap, orders[way(name, which)], pair)

    def back(name, value):
        kernel = functools.partial(back_kernel, ends[way(name, 1)])
        return start(name, 1, launch(name, kernel, sent_1, (value, *plain), short, work))

    def lead(name, total):
        kernel, pieces = functools.partial(front_kernel, ends[way(name, 0)]), (total.keep, total.other)
        return launch(name, kernel, [ranged, small, lines], (*pieces, *turned), narrow, work)

    def open_group(name, source):
        rhs, *pair = launch(
            name,
            functools.partial(rhs_kernel, ends[way(name, 0)], masks),
            [lines] + sent_0,
            (*source, *down, energy_a, energy_b),
            [every] + wide + short + spread,
            3 * work,
        )
        return rhs, start(name, 0, pair)

    def middle(name, total, led, rhs):
        before, norms, part = led
        x, scalars, image, residual, *pair = launch(
            name,
            functools.partial(first_kernel, (ends[way(name, 0)], ends[way(name, 1)]), receivers),
            [ranged, small, lines, lines] + sent_0,
            (total.keep, total.other, before, norms, part, rhs, *down),
            narrow + short,
            2 * work,
        )
        return (rhs, before, x, scalars, image, residual), start(name, 0, pair)

    def close(name, total, led, kept):
        keep, give = launch(
            name,
            functools.partial(last_kernel, ends[way(name, 1)]),
            [((2, packed, rows), f32)] * 2,
            (total.keep, total.other, *led, *kept, *turned),
            [ranged] + narrow,
            work,
        )
        return keep, swap(give, 0)

    def rounds(tag, a0, a1, b0, pending):
        step("a0" + tag, a0)
        step("a1" + tag, a1)
        b1 = back("bC" + tag, pending)
        for turn in range(2, len(chip_bits) + 1):
            end = tag + str(turn)
            step("a0" + end, a0)
            step("b0" + end, b0)
            step("b1" + end, b1)
            step("a1" + end, a1)
        led = lead("aL" + tag, a0)
        step("b0" + tag, b0)
        step("b1" + tag, b1)
        return b1, led

    rhs_a, a0 = open_group("aR", sources[0])
    a1 = back("aC", rhs_a)
    rhs_b, b0 = open_group("bR", sources[1])
    b1, led = rounds("", a0, a1, b0, rhs_b)
    kept_a, a0 = middle("aM", a1, led, rhs_a)
    a1 = back("aC.", kept_a[-1])
    led = lead("bL", b0)
    kept_b, b0 = middle("bM", b1, led, rhs_b)
    b1, led = rounds(".", a0, a1, b0, kept_b[-1])
    results = [close("aE", a1, led, kept_a)]
    led = lead("bL.", b0)
    results.append(close("bE", b1, led, kept_b))

    pieces = [piece for pair in results for piece in pair]
    columns = GROUPS * packed
    return tuple(call(functools.partial(order_kernel, own), [((2, rows, columns), f32)] * 2, pieces, [((columns, rows), f32)]))


def solution(mesh):
    count = mesh.shape["rcv"]

    def run(down_spectra, up_sources):
        return body(down_spectra, up_sources, count=count, receivers=down_spectra.shape[1] * count)

    specs = (P("cuts", "rcv", None), P("cuts", "rcv", None))
    return jax.shard_map(run, mesh=mesh, in_specs=specs, out_specs=specs, check_vma=False)
```

```python
import functools
import jax
import jax.numpy as jnp
from jax import lax
from jax.experimental import pallas as pl
from jax.experimental.pallas import tpu as pltpu
from jax.sharding import PartitionSpec as P

damping_ratio = 0.1
LANES = 128
GROUPS = 2
ORDER = {"bE": ["a1.2"], "b02": ["aC"]}
COST = {"aR": 30, "aC": 0.3, "bC": 3, "aL": 0, "aC.": 3, "bC.": 0.3, "aL.": 0, "bL.": 0}
f32 = jnp.float32
bf16 = jnp.bfloat16


def dot(left, right):
    return lax.dot_general(left, right, (((1,), (0,)), ((), ())), preferred_element_type=f32)


def parts_of(value):
    high = value.astype(bf16)
    return high, (value - high.astype(f32)).astype(bf16)


def call(kernel, outs, args, scratch=(), flops=0, in_specs=None):
    spec = pl.BlockSpec(memory_space=pltpu.VMEM)
    moved = sum(value.size * value.dtype.itemsize for value in args)
    return pl.pallas_call(
        kernel,
        out_shape=[jax.ShapeDtypeStruct(shape, dtype) for shape, dtype in outs],
        in_specs=in_specs or [spec] * len(args),
        out_specs=[spec] * len(outs),
        scratch_shapes=[pltpu.VMEM(*item) if isinstance(item, tuple) else item for item in scratch],
        cost_estimate=pl.CostEstimate(flops=flops, transcendentals=0, bytes_accessed=moved),
        compiler_params=pltpu.CompilerParams(vmem_limit_bytes=16 << 20),
    )(*args)


def split_piece(down_ref, part, at, places, high_ref, low_ref, turned_high_ref, turned_low_ref, energy_ref):
    for place in places:
        value = down_ref[part, at, place]
        rows, width = value.shape
        high, low = parts_of(value)
        high_ref[part, at, place] = high
        low_ref[part, at, place] = low
        turned_high_ref[part, place, at] = high.T
        turned_low_ref[part, place, at] = low.T
        square = jnp.sum((value * value).reshape(rows // 8, 8, width), axis=0)
        energy_ref[...] += sum(square[:, lane : lane + LANES] for lane in range(0, width, LANES))


def pieces_of(shape):
    _, rows, shots = shape
    block, width = min(rows, LANES), shots // 2
    starts = [(row, start) for row in range(0, rows, block) for start in range(0, shots, width)]
    return [(part, slice(row, row + block), slice(start, start + width)) for part in range(2) for row, start in starts]


def places_of(shots):
    width = 2 * LANES
    return [slice(start, start + width) for start in range(shots.start, shots.stop, width)]


def split_kernel(down_ref, *outs):
    outs[4][...] = jnp.zeros_like(outs[4])
    for part, at, shots in pieces_of(down_ref.shape):
        split_piece(down_ref, part, at, places_of(shots), *outs)


def fetch_split_kernel(down_ref, *refs):
    outs, (held_ref, sems) = refs[:5], refs[5:]
    copies = []
    for where in pieces_of(down_ref.shape):
        copies.append(pltpu.make_async_copy(down_ref.at[where], held_ref.at[where], sems.at[len(copies)]))
        copies[-1].start()
    outs[4][...] = jnp.zeros_like(outs[4])
    for copy, (part, at, shots) in zip(copies, pieces_of(down_ref.shape)):
        copy.wait()
        split_piece(held_ref, part, at, places_of(shots), *outs)


def split(value, from_hbm=False):
    _, rows, shots = value.shape
    plain, turned = ((2, rows, shots), bf16), ((2, shots, rows), bf16)
    outs = [plain, plain, turned, turned, ((8, LANES), f32)]
    if from_hbm:
        value = pltpu.with_memory_space_constraint(value, pltpu.HBM)
        scratch = [pltpu.VMEM(value.shape, f32), pltpu.SemaphoreType.DMA((len(pieces_of(value.shape)),))]
        specs = [pl.BlockSpec(memory_space=pltpu.HBM)]
        high, low, turned_high, turned_low, energy = call(fetch_split_kernel, outs, (value,), scratch, in_specs=specs)
    else:
        high, low, turned_high, turned_low, energy = call(split_kernel, outs, (value,))
    return (high, low), (turned_high, turned_low), energy


def stage(value_ref, first_ref, second_ref, sign):
    half = value_ref.shape[0] // 2
    real = value_ref[:half, :]
    imag = value_ref[half:, :]
    for at, (a, b) in enumerate(zip(parts_of(real), parts_of(imag))):
        base = 2 * half * at
        first_ref[base : base + half, :] = a
        first_ref[base + half : base + 2 * half, :] = b
        second_ref[base : base + half, :] = b if sign > 0 else -b
        second_ref[base + half : base + 2 * half, :] = a if sign < 0 else -a


def times(first, second, high_ref, low_ref, columns=slice(None)):
    count = first.shape[0] // 2
    total = dot(first, high_ref[0, :, columns]) + dot(second, high_ref[1, :, columns])
    low = dot(first[:count], low_ref[0, :, columns]) + dot(second[:count], low_ref[1, :, columns])
    return total[:count] + total[count:] + low


def row_squares(value):
    return jnp.sum(value * value, axis=1, keepdims=True)


def both(value):
    half = value.shape[0] // 2
    total = value[:half] + value[half:]
    return jnp.concatenate([total, total], axis=0)


def tail(*columns):
    lane = lax.broadcasted_iota(jnp.int32, (columns[0].shape[0], LANES), 1)
    out = jnp.zeros(lane.shape, f32)
    for at, column in enumerate(columns):
        out = jnp.where(lane == at, column, out)
    return out


def apply_down(x_ref, first_ref, second_ref, turned, shots=slice(None)):
    stage(x_ref, first_ref, second_ref, -1)
    first, second = first_ref[...], second_ref[...]
    count = first.shape[0] // 2
    blocks = []
    for high, low in turned:
        total = dot(first, high[0, shots, :]) + dot(second, high[1, shots, :])
        rest = dot(first[:count], low[0, shots, :]) + dot(second[:count], low[1, shots, :])
        blocks.append(total[:count] + total[count:] + rest)
    return jnp.concatenate(blocks, axis=1)


def device_bit(bit):
    return (lax.axis_index("rcv") >> bit) & 1


def project(value_ref, first_ref, second_ref, plain, columns, keep_ref, give_ref, bit, extra=None):
    stage(value_ref, first_ref, second_ref, 1)
    rows = plain[0][0].shape[1]
    half = value_ref.shape[0] // 2
    front = columns.stop - columns.start
    total = 0.0
    for block, (high, low) in enumerate(plain):
        own = slice(block * rows, (block + 1) * rows)
        total = total + times(first_ref[:, own], second_ref[:, own], high, low, columns)
    upper = device_bit(bit) == 1
    keep_ref[:, :front] = jnp.where(upper, total[half:], total[:half])
    give_ref[:, :front] = jnp.where(upper, total[:half], total[half:])
    if extra is not None:
        keep_ref[:, front:] = jnp.where(upper, extra[half:], extra[:half])
        give_ref[:, front:] = jnp.where(upper, extra[:half], extra[half:])


def collect(pieces, x_ref, bit, ends_ref=None):
    upper = device_bit(bit)
    front = x_ref.shape[1]
    for which, piece in enumerate(pieces):
        half = piece.shape[0]
        place = pl.ds(pl.multiple_of((upper ^ which) * half, half), half)
        x_ref[place, :] = piece[:, :front]
        if ends_ref is not None:
            ends_ref[place, :] = piece[:, front:]


def pairs(refs):
    return tuple((refs[at], refs[at + 1]) for at in range(0, len(refs), 2))


def rhs_kernel(bit, masks, *refs):
    sources, refs = refs[: len(masks)], refs[len(masks) :]
    down, refs = refs[:8], refs[8:]
    (ea, eb), (rhs_ref, *outs), (x_ref, f0, s0, f1, s1, *spread) = refs[:2], refs[2:5], refs[5:]
    half = x_ref.shape[0] // 2
    own = sources[0].shape[1]
    chip = lax.axis_index("rcv") >> 1
    for mask, source in zip(masks, sources):
        for part, value in enumerate((source[0], -source[1])):
            if spread:
                spread[0][part * half // own + (chip ^ mask)] = value
            else:
                x_ref[pl.ds(pl.multiple_of(part * half + (chip ^ mask) * own, own), own), :] = value
    for at in range(2 * half // own if spread else 0):
        x_ref[at * own : (at + 1) * own, :] = spread[0][at]
    rhs_ref[...] = apply_down(x_ref, f0, s0, pairs(down[4:]))
    energy = jnp.full((2 * half, 1), jnp.sum(ea[...] + eb[...]), f32)
    extra = tail(row_squares(rhs_ref[...]), energy)
    front = outs[0].shape[1] - LANES
    project(rhs_ref, f1, s1, pairs(down[:4]), slice(0, front), *outs, bit, extra)


def back_kernel(bit, *refs):
    value_ref, down, outs, scratch = refs[0], refs[1:5], refs[5:7], refs[7:]
    shots = down[0].shape[2]
    project(value_ref, *scratch, pairs(down), slice(shots - outs[0].shape[1], shots), *outs, bit)


def front_kernel(bit, *refs):
    pieces, turned, (x_ref, ends_ref, image_ref), scratch = refs[:2], refs[2:6], refs[6:9], refs[9:]
    collect(pieces, x_ref, bit, ends_ref)
    image_ref[...] = apply_down(x_ref, *scratch, pairs(turned), slice(0, x_ref.shape[1]))


def first_kernel(bits, receivers, *refs):
    pieces, (before_ref, ends_ref, part_ref, rhs_ref, *refs) = refs[:2], refs[2:]
    down, refs = refs[:8], refs[8:]
    (x_ref, scalar_ref, image_ref, residual_ref, *outs), (f0, s0, f1, s1) = refs[:6], refs[6:]
    front = before_ref.shape[1]
    collect(pieces, x_ref, bits[1])
    norm = both(ends_ref[:, 0:1])
    damping = damping_ratio * ends_ref[:, 1:2] / receivers
    image = part_ref[...] + apply_down(x_ref, f0, s0, pairs(down[4:]), slice(front, None)) + damping * rhs_ref[...]
    image_ref[...] = image
    alpha = norm / (both(row_squares(before_ref[...]) + row_squares(x_ref[...])) + damping * norm)
    residual = rhs_ref[...] - alpha * image
    residual_ref[...] = residual
    scalar_ref[...] = tail(norm, damping, alpha)
    project(residual_ref, f1, s1, pairs(down[:4]), slice(0, front), *outs, bits[0], tail(row_squares(residual)))


def last_kernel(bit, *refs):
    pieces, (a_ref, ends_ref, part_ref, rhs_ref, before_a, before_b, scalar_ref, image_ref, residual_ref) = refs[:2], refs[2:11]
    turned, (keep_ref, give_ref, x_ref, *scratch) = refs[11:15], refs[15:]
    front = a_ref.shape[1]
    collect(pieces, x_ref, bit)
    following = both(ends_ref[:, 0:1])
    norm = scalar_ref[:, 0:1]
    damping = scalar_ref[:, 1:2]
    alpha = scalar_ref[:, 2:3]
    beta = following / norm
    residual = residual_ref[...]
    image = part_ref[...] + apply_down(x_ref, *scratch, pairs(turned), slice(front, None))
    image = image + beta * image_ref[...] + damping * residual
    squares = row_squares(a_ref[...] + beta * before_a[...]) + row_squares(x_ref[...] + beta * before_b[...])
    curvature = both(squares) + damping * (following + beta * following)
    alpha_next = following / curvature
    rhs = rhs_ref[...]
    found = alpha * rhs + alpha_next * (residual + beta * rhs)
    left = residual - alpha_next * image
    rows = turned[0].shape[2]
    keep_ref[0] = found[:, :rows]
    keep_ref[1] = left[:, :rows]
    give_ref[0] = found[:, rows:]
    give_ref[1] = left[:, rows:]


def order_kernel(own, *refs):
    pieces, (*outs, x_ref) = refs[: 2 * GROUPS], refs[2 * GROUPS :]
    upper = device_bit(0) == 1
    chips = pieces[0].shape[1] // (2 * own)
    for which, out_ref in enumerate(outs):
        for part in range(2):
            for chip in range(chips):
                source = pl.ds((part * chips + chip) * own, own)
                for group in range(GROUPS):
                    mine = pieces[2 * group][which, source, :]
                    other = pieces[2 * group + 1][which, source, :]
                    base = (2 * chip * GROUPS + group) * own
                    x_ref[base : base + own, :] = jnp.where(upper, other, mine)
                    base += GROUPS * own
                    x_ref[base : base + own, :] = jnp.where(upper, mine, other)
            out_ref[part] = x_ref[...].T


class Sum:
    def __init__(self, swap, order, pair):
        self.swap, self.order, self.at = swap, order, 0
        self.keep, give = pair
        self.other = swap(give, order[0])

    def step(self):
        self.at += 1
        self.keep = self.keep + self.other
        self.other = self.swap(self.keep, self.order[self.at % len(self.order)])


def body(down_spectra, up_sources, *, count, receivers):
    chip_bits = list(range(1, count.bit_length() - 1))
    orders = (chip_bits, chip_bits[::-1])
    ends = (chip_bits[0], chip_bits[-1])
    rows, shots = down_spectra.shape[1:]
    own = up_sources.shape[1] // GROUPS
    chips = count // 2
    packed = 2 * chips * own
    front = shots // 2

    def swap(value, bit):
        return lax.ppermute(value, "rcv", [(at, at ^ (1 << bit)) for at in range(count)])

    def jump(value, mask):
        return lax.ppermute(value, "rcv", [(at, at ^ (mask << 1)) for at in range(count)])

    other_down = swap(down_spectra, 0)
    masks = sorted(range(chips), key=lambda mask: mask.bit_count())
    sources = []
    for group in range(GROUPS):
        part = up_sources[:, group * own : (group + 1) * own]
        sources.append([jump(part, mask) if mask else part for mask in masks])
    plain_a, turned_a, energy_a = split(down_spectra, from_hbm=True)
    plain_b, turned_b, energy_b = split(other_down)
    turned = (*turned_a, *turned_b)
    down = (*plain_a, *plain_b, *turned)

    wide = [((2 * packed, shots), bf16)] * 2
    narrow = [((2 * packed, front), bf16)] * 2
    short = [((2 * packed, 2 * rows), bf16)] * 2
    lines = ((packed, 2 * rows), f32)
    every = ((packed, shots), f32)
    ranged = ((packed, front), f32)
    small = ((packed, LANES), f32)
    work = 2 * 2 * 2 * (3 * packed) * rows * shots
    sent_0 = [((packed // 2, front + LANES), f32)] * 2
    sent_1 = [((packed // 2, front), f32)] * 2
    spread = [((packed // own, own, shots), f32)] if own % 8 else []
    plain = (*plain_a, *plain_b)

    done = {}

    def after(name, *values):
        for earlier in ORDER.get(name, ()):
            values = lax.optimization_barrier((done[earlier], *values))[1:]
        return values

    def launch(name, kernel, outs, args, scratch, flops):
        first, *rest = args
        results = call(kernel, outs, (*after(name, first), *rest), scratch, int(flops * COST.get(name, 1)))
        done[name] = results[0]
        return results

    def step(name, total):
        (total.keep,) = after(name, total.keep)
        total.step()
        done[name] = total.keep

    def way(name, which):
        return which ^ (name[0] == "b")

    def start(name, which, pair):
        return Sum(swap, orders[way(name, which)], pair)

    def back(name, value):
        kernel = functools.partial(back_kernel, ends[way(name, 1)])
        return start(name, 1, launch(name, kernel, sent_1, (value, *plain), short, work))

    def lead(name, total):
        kernel, pieces = functools.partial(front_kernel, ends[way(name, 0)]), (total.keep, total.other)
        return launch(name, kernel, [ranged, small, lines], (*pieces, *turned), narrow, work)

    def open_group(name, source):
        rhs, *pair = launch(
            name,
            functools.partial(rhs_kernel, ends[way(name, 0)], masks),
            [lines] + sent_0,
            (*source, *down, energy_a, energy_b),
            [every] + wide + short + spread,
            3 * work,
        )
        return rhs, start(name, 0, pair)

    def middle(name, total, led, rhs):
        before, norms, part = led
        x, scalars, image, residual, *pair = launch(
            name,
            functools.partial(first_kernel, (ends[way(name, 0)], ends[way(name, 1)]), receivers),
            [ranged, small, lines, lines] + sent_0,
            (total.keep, total.other, before, norms, part, rhs, *down),
            narrow + short,
            2 * work,
        )
        return (rhs, before, x, scalars, image, residual), start(name, 0, pair)

    def close(name, total, led, kept):
        keep, give = launch(
            name,
            functools.partial(last_kernel, ends[way(name, 1)]),
            [((2, packed, rows), f32)] * 2,
            (total.keep, total.other, *led, *kept, *turned),
            [ranged] + narrow,
            work,
        )
        return keep, swap(give, 0)

    def rounds(tag, a0, a1, b0, pending):
        step("a0" + tag, a0)
        step("a1" + tag, a1)
        b1 = back("bC" + tag, pending)
        for turn in range(2, len(chip_bits) + 1):
            end = tag + str(turn)
            step("a0" + end, a0)
            step("b0" + end, b0)
            step("b1" + end, b1)
            step("a1" + end, a1)
        led = lead("aL" + tag, a0)
        step("b0" + tag, b0)
        step("b1" + tag, b1)
        return b1, led

    rhs_a, a0 = open_group("aR", sources[0])
    a1 = back("aC", rhs_a)
    rhs_b, b0 = open_group("bR", sources[1])
    b1, led = rounds("", a0, a1, b0, rhs_b)
    kept_a, a0 = middle("aM", a1, led, rhs_a)
    a1 = back("aC.", kept_a[-1])
    led = lead("bL", b0)
    kept_b, b0 = middle("bM", b1, led, rhs_b)
    b1, led = rounds(".", a0, a1, b0, kept_b[-1])
    results = [close("aE", a1, led, kept_a)]
    led = lead("bL.", b0)
    results.append(close("bE", b1, led, kept_b))

    pieces = [piece for pair in results for piece in pair]
    columns = GROUPS * packed
    return tuple(call(functools.partial(order_kernel, own), [((2, rows, columns), f32)] * 2, pieces, [((columns, rows), f32)]))


def solution(mesh):
    count = mesh.shape["rcv"]

    def run(down_spectra, up_sources):
        return body(down_spectra, up_sources, count=count, receivers=down_spectra.shape[1] * count)

    specs = (P("cuts", "rcv", None), P("cuts", "rcv", None))
    return jax.shard_map(run, mesh=mesh, in_specs=specs, out_specs=specs, check_vma=False)
```

```python
import functools
import jax
import jax.numpy as jnp
from jax import lax
from jax.experimental import pallas as pl
from jax.experimental.pallas import tpu as pltpu
from jax.sharding import PartitionSpec as P

damping_ratio = 0.1
LANES = 128
GROUPS = 2
ORDER = {'bE': ['a1.2']}
COST = {'bC.': 0.3, 'aL.': 0, 'aR': 30, 'bM': 10, 'bL.': 0, 'bC': 0, 'aC': 0.3, 'aC.': 3, 'aL': 0}
f32 = jnp.float32
bf16 = jnp.bfloat16


def dot(left, right):
    return lax.dot_general(left, right, (((1,), (0,)), ((), ())), preferred_element_type=f32)


def parts_of(value):
    high = value.astype(bf16)
    return high, (value - high.astype(f32)).astype(bf16)


def call(kernel, outs, args, scratch=(), flops=0, grid=(), in_specs=None):
    spec = pl.BlockSpec(memory_space=pltpu.VMEM)
    moved = sum(value.size * value.dtype.itemsize for value in args)
    return pl.pallas_call(
        kernel,
        out_shape=[jax.ShapeDtypeStruct(shape, dtype) for shape, dtype in outs],
        grid=grid,
        in_specs=in_specs or [spec] * len(args),
        out_specs=[spec] * len(outs),
        scratch_shapes=[pltpu.VMEM(shape, dtype) for shape, dtype in scratch],
        cost_estimate=pl.CostEstimate(flops=flops, transcendentals=0, bytes_accessed=moved),
        compiler_params=pltpu.CompilerParams(vmem_limit_bytes=16 << 20),
    )(*args)


def split_kernel(real_ref, imag_ref, high_ref, low_ref, turned_high_ref, turned_low_ref, energy_ref):
    rows, shots = real_ref.shape[1:]
    step, chunk = pl.program_id(0), pl.program_id(1)
    width = 2 * LANES
    at = slice(None) if rows == high_ref.shape[1] else pl.ds(pl.multiple_of(step * rows, rows), rows)

    @pl.when((step == 0) & (chunk == 0))
    def _():
        energy_ref[...] = jnp.zeros_like(energy_ref)

    for part, ref in enumerate((real_ref, imag_ref)):
        for start in range(0, shots, width):
            value = ref[0, :, start : start + width]
            place = pl.ds(pl.multiple_of(chunk * shots + start, width), width)
            high, low = parts_of(value)
            high_ref[part, at, place] = high
            low_ref[part, at, place] = low
            turned_high_ref[part, place, at] = high.T
            turned_low_ref[part, place, at] = low.T
            square = jnp.sum((value * value).reshape(rows // 8, 8, width), axis=0)
            energy_ref[...] += sum(square[:, lane : lane + LANES] for lane in range(0, width, LANES))


def split(value):
    _, rows, shots = value.shape
    block, chunks = min(rows, LANES), 2
    plain, turned = ((2, rows, shots), bf16), ((2, shots, rows), bf16)
    high, low, turned_high, turned_low, energy = call(
        split_kernel,
        [plain, plain, turned, turned, ((8, LANES), f32)],
        (value, value),
        grid=(rows // block, chunks),
        in_specs=[
            pl.BlockSpec((1, block, shots // chunks), lambda step, chunk: (0, step, chunk)),
            pl.BlockSpec((1, block, shots // chunks), lambda step, chunk: (1, step, chunk)),
        ],
    )
    return (high, low), (turned_high, turned_low), energy


def stage(value_ref, first_ref, second_ref, sign):
    half = value_ref.shape[0] // 2
    real = value_ref[:half, :]
    imag = value_ref[half:, :]
    for at, (a, b) in enumerate(zip(parts_of(real), parts_of(imag))):
        base = 2 * half * at
        first_ref[base : base + half, :] = a
        first_ref[base + half : base + 2 * half, :] = b
        second_ref[base : base + half, :] = b if sign > 0 else -b
        second_ref[base + half : base + 2 * half, :] = a if sign < 0 else -a


def times(first, second, high_ref, low_ref, columns=slice(None)):
    count = first.shape[0] // 2
    total = dot(first, high_ref[0, :, columns]) + dot(second, high_ref[1, :, columns])
    low = dot(first[:count], low_ref[0, :, columns]) + dot(second[:count], low_ref[1, :, columns])
    return total[:count] + total[count:] + low


def row_squares(value):
    return jnp.sum(value * value, axis=1, keepdims=True)


def both(value):
    half = value.shape[0] // 2
    total = value[:half] + value[half:]
    return jnp.concatenate([total, total], axis=0)


def tail(*columns):
    lane = lax.broadcasted_iota(jnp.int32, (columns[0].shape[0], LANES), 1)
    out = jnp.zeros(lane.shape, f32)
    for at, column in enumerate(columns):
        out = jnp.where(lane == at, column, out)
    return out


def apply_down(x_ref, first_ref, second_ref, turned, shots=slice(None)):
    stage(x_ref, first_ref, second_ref, -1)
    first, second = first_ref[...], second_ref[...]
    count = first.shape[0] // 2
    blocks = []
    for high, low in turned:
        total = dot(first, high[0, shots, :]) + dot(second, high[1, shots, :])
        rest = dot(first[:count], low[0, shots, :]) + dot(second[:count], low[1, shots, :])
        blocks.append(total[:count] + total[count:] + rest)
    return jnp.concatenate(blocks, axis=1)


def device_bit(bit):
    return (lax.axis_index("rcv") >> bit) & 1


def project(value_ref, first_ref, second_ref, plain, columns, keep_ref, give_ref, bit, extra=None):
    stage(value_ref, first_ref, second_ref, 1)
    rows = plain[0][0].shape[1]
    half = value_ref.shape[0] // 2
    front = columns.stop - columns.start
    total = 0.0
    for block, (high, low) in enumerate(plain):
        own = slice(block * rows, (block + 1) * rows)
        total = total + times(first_ref[:, own], second_ref[:, own], high, low, columns)
    upper = device_bit(bit) == 1
    keep_ref[:, :front] = jnp.where(upper, total[half:], total[:half])
    give_ref[:, :front] = jnp.where(upper, total[:half], total[half:])
    if extra is not None:
        keep_ref[:, front:] = jnp.where(upper, extra[half:], extra[:half])
        give_ref[:, front:] = jnp.where(upper, extra[:half], extra[half:])


def collect(pieces, x_ref, bit, ends_ref=None):
    upper = device_bit(bit)
    front = x_ref.shape[1]
    for which, piece in enumerate(pieces):
        half = piece.shape[0]
        place = pl.ds(pl.multiple_of((upper ^ which) * half, half), half)
        x_ref[place, :] = piece[:, :front]
        if ends_ref is not None:
            ends_ref[place, :] = piece[:, front:]


def pairs(refs):
    return tuple((refs[at], refs[at + 1]) for at in range(0, len(refs), 2))


def rhs_kernel(bit, masks, *refs):
    sources, refs = refs[: len(masks)], refs[len(masks) :]
    down, refs = refs[:8], refs[8:]
    (ea, eb), (rhs_ref, *outs), (x_ref, f0, s0, f1, s1, *spread) = refs[:2], refs[2:5], refs[5:]
    half = x_ref.shape[0] // 2
    own = sources[0].shape[1]
    chip = lax.axis_index("rcv") >> 1
    for mask, source in zip(masks, sources):
        for part, value in enumerate((source[0], -source[1])):
            if spread:
                spread[0][part * half // own + (chip ^ mask)] = value
            else:
                x_ref[pl.ds(pl.multiple_of(part * half + (chip ^ mask) * own, own), own), :] = value
    for at in range(2 * half // own if spread else 0):
        x_ref[at * own : (at + 1) * own, :] = spread[0][at]
    rhs_ref[...] = apply_down(x_ref, f0, s0, pairs(down[4:]))
    energy = jnp.full((2 * half, 1), jnp.sum(ea[...] + eb[...]), f32)
    extra = tail(row_squares(rhs_ref[...]), energy)
    front = outs[0].shape[1] - LANES
    project(rhs_ref, f1, s1, pairs(down[:4]), slice(0, front), *outs, bit, extra)


def back_kernel(bit, *refs):
    value_ref, down, outs, scratch = refs[0], refs[1:5], refs[5:7], refs[7:]
    shots = down[0].shape[2]
    project(value_ref, *scratch, pairs(down), slice(shots - outs[0].shape[1], shots), *outs, bit)


def front_kernel(bit, *refs):
    pieces, turned, (x_ref, ends_ref, image_ref), scratch = refs[:2], refs[2:6], refs[6:9], refs[9:]
    collect(pieces, x_ref, bit, ends_ref)
    image_ref[...] = apply_down(x_ref, *scratch, pairs(turned), slice(0, x_ref.shape[1]))


def first_kernel(bits, receivers, *refs):
    pieces, (before_ref, ends_ref, part_ref, rhs_ref, *refs) = refs[:2], refs[2:]
    down, refs = refs[:8], refs[8:]
    (x_ref, scalar_ref, image_ref, residual_ref, *outs), (f0, s0, f1, s1) = refs[:6], refs[6:]
    front = before_ref.shape[1]
    collect(pieces, x_ref, bits[1])
    norm = both(ends_ref[:, 0:1])
    damping = damping_ratio * ends_ref[:, 1:2] / receivers
    image = part_ref[...] + apply_down(x_ref, f0, s0, pairs(down[4:]), slice(front, None)) + damping * rhs_ref[...]
    image_ref[...] = image
    alpha = norm / (both(row_squares(before_ref[...]) + row_squares(x_ref[...])) + damping * norm)
    residual = rhs_ref[...] - alpha * image
    residual_ref[...] = residual
    scalar_ref[...] = tail(norm, damping, alpha)
    project(residual_ref, f1, s1, pairs(down[:4]), slice(0, front), *outs, bits[0], tail(row_squares(residual)))


def last_kernel(bit, side, *refs):
    pieces, (a_ref, ends_ref, part_ref, rhs_ref, before_a, before_b, scalar_ref, image_ref, residual_ref) = refs[:2], refs[2:11]
    turned, (out_ref, x_ref, *scratch) = refs[11:13], refs[13:]
    rows = turned[0].shape[2]
    lines = slice(side * rows, (side + 1) * rows)
    front = a_ref.shape[1]
    collect(pieces, x_ref, bit)
    following = both(ends_ref[:, 0:1])
    norm = scalar_ref[:, 0:1]
    damping = scalar_ref[:, 1:2]
    alpha = scalar_ref[:, 2:3]
    beta = following / norm
    residual = residual_ref[:, lines]
    image = part_ref[:, lines] + apply_down(x_ref, *scratch, pairs(turned), slice(front, None))
    image = image + beta * image_ref[:, lines] + damping * residual
    squares = row_squares(a_ref[...] + beta * before_a[...]) + row_squares(x_ref[...] + beta * before_b[...])
    curvature = both(squares) + damping * (following + beta * following)
    alpha_next = following / curvature
    rhs = rhs_ref[:, lines]
    found = alpha * rhs + alpha_next * (residual + beta * rhs)
    left = residual - alpha_next * image
    out_ref[0] = found
    out_ref[1] = left


def whole_kernel(bit, *refs):
    pieces, (a_ref, ends_ref, part_ref, rhs_ref, before_a, before_b, scalar_ref, image_ref, residual_ref) = refs[:2], refs[2:11]
    turned, (keep_ref, give_ref, x_ref, *scratch) = refs[11:15], refs[15:]
    front = a_ref.shape[1]
    collect(pieces, x_ref, bit)
    following = both(ends_ref[:, 0:1])
    norm = scalar_ref[:, 0:1]
    damping = scalar_ref[:, 1:2]
    alpha = scalar_ref[:, 2:3]
    beta = following / norm
    residual = residual_ref[...]
    image = part_ref[...] + apply_down(x_ref, *scratch, pairs(turned), slice(front, None))
    image = image + beta * image_ref[...] + damping * residual
    squares = row_squares(a_ref[...] + beta * before_a[...]) + row_squares(x_ref[...] + beta * before_b[...])
    curvature = both(squares) + damping * (following + beta * following)
    alpha_next = following / curvature
    rhs = rhs_ref[...]
    found = alpha * rhs + alpha_next * (residual + beta * rhs)
    left = residual - alpha_next * image
    rows = turned[0].shape[2]
    keep_ref[0] = found[:, :rows]
    keep_ref[1] = left[:, :rows]
    give_ref[0] = found[:, rows:]
    give_ref[1] = left[:, rows:]


def order_kernel(own, *refs):
    pieces, (*outs, x_ref) = refs[: 2 * GROUPS], refs[2 * GROUPS :]
    upper = device_bit(0) == 1
    chips = pieces[0].shape[1] // (2 * own)
    for which, out_ref in enumerate(outs):
        for part in range(2):
            for chip in range(chips):
                source = pl.ds((part * chips + chip) * own, own)
                for group in range(GROUPS):
                    mine = pieces[2 * group][which, source, :]
                    other = pieces[2 * group + 1][which, source, :]
                    base = (2 * chip * GROUPS + group) * own
                    x_ref[base : base + own, :] = jnp.where(upper, other, mine)
                    base += GROUPS * own
                    x_ref[base : base + own, :] = jnp.where(upper, mine, other)
            out_ref[part] = x_ref[...].T


class Sum:
    def __init__(self, swap, order, pair):
        self.swap, self.order, self.at = swap, order, 0
        self.keep, give = pair
        self.other = swap(give, order[0])

    def step(self):
        self.at += 1
        self.keep = self.keep + self.other
        self.other = self.swap(self.keep, self.order[self.at % len(self.order)])


def body(down_spectra, up_sources, *, count, receivers):
    chip_bits = list(range(1, count.bit_length() - 1))
    orders = (chip_bits, chip_bits[::-1])
    ends = (chip_bits[0], chip_bits[-1])
    rows, shots = down_spectra.shape[1:]
    own = up_sources.shape[1] // GROUPS
    chips = count // 2
    packed = 2 * chips * own
    front = shots // 2

    def swap(value, bit):
        return lax.ppermute(value, "rcv", [(at, at ^ (1 << bit)) for at in range(count)])

    def jump(value, mask):
        return lax.ppermute(value, "rcv", [(at, at ^ (mask << 1)) for at in range(count)])

    other_down = swap(down_spectra, 0)
    masks = sorted(range(chips), key=lambda mask: mask.bit_count())
    sources = []
    for group in range(GROUPS):
        part = up_sources[:, group * own : (group + 1) * own]
        sources.append([jump(part, mask) if mask else part for mask in masks])
    plain_a, turned_a, energy_a = split(pltpu.with_memory_space_constraint(down_spectra, pltpu.HBM))
    plain_b, turned_b, energy_b = split(other_down)
    turned = (*turned_a, *turned_b)
    down = (*plain_a, *plain_b, *turned)

    wide = [((2 * packed, shots), bf16)] * 2
    narrow = [((2 * packed, front), bf16)] * 2
    short = [((2 * packed, 2 * rows), bf16)] * 2
    lines = ((packed, 2 * rows), f32)
    every = ((packed, shots), f32)
    ranged = ((packed, front), f32)
    small = ((packed, LANES), f32)
    work = 2 * 2 * 2 * (3 * packed) * rows * shots
    sent_0 = [((packed // 2, front + LANES), f32)] * 2
    sent_1 = [((packed // 2, front), f32)] * 2
    spread = [((packed // own, own, shots), f32)] if own % 8 else []
    plain = (*plain_a, *plain_b)

    done = {}

    def after(name, *values):
        for earlier in ORDER.get(name, ()):
            values = lax.optimization_barrier((done[earlier], *values))[1:]
        return values

    def launch(name, kernel, outs, args, scratch, flops):
        first, *rest = args
        results = call(kernel, outs, (*after(name, first), *rest), scratch, int(flops * COST.get(name, 1)))
        done[name] = results[0]
        return results

    def step(name, total):
        (total.keep,) = after(name, total.keep)
        total.step()
        done[name] = total.keep

    def way(name, which):
        return which ^ (name[0] == "b")

    def start(name, which, pair):
        return Sum(swap, orders[way(name, which)], pair)

    def back(name, value):
        kernel = functools.partial(back_kernel, ends[way(name, 1)])
        return start(name, 1, launch(name, kernel, sent_1, (value, *plain), short, work))

    def lead(name, total):
        kernel, pieces = functools.partial(front_kernel, ends[way(name, 0)]), (total.keep, total.other)
        return launch(name, kernel, [ranged, small, lines], (*pieces, *turned), narrow, work)

    def open_group(name, source):
        rhs, *pair = launch(
            name,
            functools.partial(rhs_kernel, ends[way(name, 0)], masks),
            [lines] + sent_0,
            (*source, *down, energy_a, energy_b),
            [every] + wide + short + spread,
            3 * work,
        )
        return rhs, start(name, 0, pair)

    def middle(name, total, led, rhs):
        before, norms, part = led
        x, scalars, image, residual, *pair = launch(
            name,
            functools.partial(first_kernel, (ends[way(name, 0)], ends[way(name, 1)]), receivers),
            [ranged, small, lines, lines] + sent_0,
            (total.keep, total.other, before, norms, part, rhs, *down),
            narrow + short,
            2 * work,
        )
        return (rhs, before, x, scalars, image, residual), start(name, 0, pair)

    def close(name, total, led, kept):
        if name[0] == "a":
            keep, give = launch(
                name,
                functools.partial(whole_kernel, ends[way(name, 1)]),
                [((2, packed, rows), f32)] * 2,
                (total.keep, total.other, *led, *kept, *turned),
                [ranged] + narrow,
                work,
            )
            return keep, swap(give, 0)
        results = []
        for side in (1, 0):
            (piece,) = call(
                functools.partial(last_kernel, ends[way(name, 1)], side),
                [((2, packed, rows), f32)],
                (*after(name, total.keep), total.other, *led, *kept, *turned[2 * side : 2 * side + 2]),
                [ranged] + narrow,
                int(work // 2),
            )
            results.append(piece)
        give, keep = results
        return keep, swap(give, 0)

    def rounds(tag, a0, a1, b0, pending):
        step("a0" + tag, a0)
        step("a1" + tag, a1)
        b1 = back("bC" + tag, pending)
        for turn in range(2, len(chip_bits) + 1):
            end = tag + str(turn)
            step("a0" + end, a0)
            step("b0" + end, b0)
            step("b1" + end, b1)
            step("a1" + end, a1)
        led = lead("aL" + tag, a0)
        step("b0" + tag, b0)
        step("b1" + tag, b1)
        return b1, led

    rhs_a, a0 = open_group("aR", sources[0])
    a1 = back("aC", rhs_a)
    rhs_b, b0 = open_group("bR", sources[1])
    b1, led = rounds("", a0, a1, b0, rhs_b)
    kept_a, a0 = middle("aM", a1, led, rhs_a)
    a1 = back("aC.", kept_a[-1])
    led = lead("bL", b0)
    kept_b, b0 = middle("bM", b1, led, rhs_b)
    b1, led = rounds(".", a0, a1, b0, kept_b[-1])
    results = [close("aE", a1, led, kept_a)]
    led = lead("bL.", b0)
    results.append(close("bE", b1, led, kept_b))

    pieces = [piece for pair in results for piece in pair]
    columns = GROUPS * packed
    return tuple(call(functools.partial(order_kernel, own), [((2, rows, columns), f32)] * 2, pieces, [((columns, rows), f32)]))


def solution(mesh):
    count = mesh.shape["rcv"]

    def run(down_spectra, up_sources):
        return body(down_spectra, up_sources, count=count, receivers=down_spectra.shape[1] * count)

    specs = (P("cuts", "rcv", None), P("cuts", "rcv", None))
    return jax.shard_map(run, mesh=mesh, in_specs=specs, out_specs=specs, check_vma=False)
```

```python
import functools
import jax
import jax.numpy as jnp
from jax import lax
from jax.experimental import pallas as pl
from jax.experimental.pallas import tpu as pltpu
from jax.sharding import PartitionSpec as P

damping_ratio = 0.1
LANES = 128
GROUPS = 2
ORDER = {"b02": ["aC"]}
COST = {"aR": 30, "aC": 0.3, "bC": 3, "aL": 0, "aM": 30, "aC.": 3, "bC.": 0.3, "aL.": 0, "bL.": 0}
f32 = jnp.float32
bf16 = jnp.bfloat16


def dot(left, right):
    return lax.dot_general(left, right, (((1,), (0,)), ((), ())), preferred_element_type=f32)


def parts_of(value):
    high = value.astype(bf16)
    return high, (value - high.astype(f32)).astype(bf16)


def call(kernel, outs, args, scratch=(), flops=0, grid=(), in_specs=None):
    spec = pl.BlockSpec(memory_space=pltpu.VMEM)
    moved = sum(value.size * value.dtype.itemsize for value in args)
    return pl.pallas_call(
        kernel,
        out_shape=[jax.ShapeDtypeStruct(shape, dtype) for shape, dtype in outs],
        grid=grid,
        in_specs=in_specs or [spec] * len(args),
        out_specs=[spec] * len(outs),
        scratch_shapes=[pltpu.VMEM(shape, dtype) for shape, dtype in scratch],
        cost_estimate=pl.CostEstimate(flops=flops, transcendentals=0, bytes_accessed=moved),
        compiler_params=pltpu.CompilerParams(vmem_limit_bytes=16 << 20),
    )(*args)


def split_kernel(real_ref, imag_ref, high_ref, low_ref, turned_high_ref, turned_low_ref, energy_ref):
    rows, shots = real_ref.shape[1:]
    step, chunk = pl.program_id(0), pl.program_id(1)
    width = 2 * LANES
    at = slice(None) if rows == high_ref.shape[1] else pl.ds(pl.multiple_of(step * rows, rows), rows)

    @pl.when((step == 0) & (chunk == 0))
    def _():
        energy_ref[...] = jnp.zeros_like(energy_ref)

    for part, ref in enumerate((real_ref, imag_ref)):
        for start in range(0, shots, width):
            value = ref[0, :, start : start + width]
            place = pl.ds(pl.multiple_of(chunk * shots + start, width), width)
            high, low = parts_of(value)
            high_ref[part, at, place] = high
            low_ref[part, at, place] = low
            turned_high_ref[part, place, at] = high.T
            turned_low_ref[part, place, at] = low.T
            square = jnp.sum((value * value).reshape(rows // 8, 8, width), axis=0)
            energy_ref[...] += sum(square[:, lane : lane + LANES] for lane in range(0, width, LANES))


def split(value):
    _, rows, shots = value.shape
    block, chunks = min(rows, LANES), 2
    plain, turned = ((2, rows, shots), bf16), ((2, shots, rows), bf16)
    high, low, turned_high, turned_low, energy = call(
        split_kernel,
        [plain, plain, turned, turned, ((8, LANES), f32)],
        (value, value),
        grid=(rows // block, chunks),
        in_specs=[
            pl.BlockSpec((1, block, shots // chunks), lambda step, chunk: (0, step, chunk)),
            pl.BlockSpec((1, block, shots // chunks), lambda step, chunk: (1, step, chunk)),
        ],
    )
    return (high, low), (turned_high, turned_low), energy


def stage(value_ref, first_ref, second_ref, sign):
    half = value_ref.shape[0] // 2
    real = value_ref[:half, :]
    imag = value_ref[half:, :]
    for at, (a, b) in enumerate(zip(parts_of(real), parts_of(imag))):
        base = 2 * half * at
        first_ref[base : base + half, :] = a
        first_ref[base + half : base + 2 * half, :] = b
        second_ref[base : base + half, :] = b if sign > 0 else -b
        second_ref[base + half : base + 2 * half, :] = a if sign < 0 else -a


def times(first, second, high_ref, low_ref, columns=slice(None)):
    count = first.shape[0] // 2
    total = dot(first, high_ref[0, :, columns]) + dot(second, high_ref[1, :, columns])
    low = dot(first[:count], low_ref[0, :, columns]) + dot(second[:count], low_ref[1, :, columns])
    return total[:count] + total[count:] + low


def row_squares(value):
    return jnp.sum(value * value, axis=1, keepdims=True)


def both(value):
    half = value.shape[0] // 2
    total = value[:half] + value[half:]
    return jnp.concatenate([total, total], axis=0)


def tail(*columns):
    lane = lax.broadcasted_iota(jnp.int32, (columns[0].shape[0], LANES), 1)
    out = jnp.zeros(lane.shape, f32)
    for at, column in enumerate(columns):
        out = jnp.where(lane == at, column, out)
    return out


def apply_down(x_ref, first_ref, second_ref, turned, shots=slice(None)):
    stage(x_ref, first_ref, second_ref, -1)
    first, second = first_ref[...], second_ref[...]
    count = first.shape[0] // 2
    blocks = []
    for high, low in turned:
        total = dot(first, high[0, shots, :]) + dot(second, high[1, shots, :])
        rest = dot(first[:count], low[0, shots, :]) + dot(second[:count], low[1, shots, :])
        blocks.append(total[:count] + total[count:] + rest)
    return jnp.concatenate(blocks, axis=1)


def device_bit(bit):
    return (lax.axis_index("rcv") >> bit) & 1


def project(value_ref, first_ref, second_ref, plain, columns, keep_ref, give_ref, bit, extra=None):
    stage(value_ref, first_ref, second_ref, 1)
    rows = plain[0][0].shape[1]
    half = value_ref.shape[0] // 2
    front = columns.stop - columns.start
    total = 0.0
    for block, (high, low) in enumerate(plain):
        own = slice(block * rows, (block + 1) * rows)
        total = total + times(first_ref[:, own], second_ref[:, own], high, low, columns)
    upper = device_bit(bit) == 1
    keep_ref[:, :front] = jnp.where(upper, total[half:], total[:half])
    give_ref[:, :front] = jnp.where(upper, total[:half], total[half:])
    if extra is not None:
        keep_ref[:, front:] = jnp.where(upper, extra[half:], extra[:half])
        give_ref[:, front:] = jnp.where(upper, extra[:half], extra[half:])


def collect(pieces, x_ref, bit, ends_ref=None):
    upper = device_bit(bit)
    front = x_ref.shape[1]
    for which, piece in enumerate(pieces):
        half = piece.shape[0]
        place = pl.ds(pl.multiple_of((upper ^ which) * half, half), half)
        x_ref[place, :] = piece[:, :front]
        if ends_ref is not None:
            ends_ref[place, :] = piece[:, front:]


def pairs(refs):
    return tuple((refs[at], refs[at + 1]) for at in range(0, len(refs), 2))


def rhs_kernel(bit, masks, *refs):
    sources, refs = refs[: len(masks)], refs[len(masks) :]
    down, refs = refs[:8], refs[8:]
    (ea, eb), (rhs_ref, *outs), (x_ref, f0, s0, f1, s1, *spread) = refs[:2], refs[2:5], refs[5:]
    half = x_ref.shape[0] // 2
    own = sources[0].shape[1]
    chip = lax.axis_index("rcv") >> 1
    for mask, source in zip(masks, sources):
        for part, value in enumerate((source[0], -source[1])):
            if spread:
                spread[0][part * half // own + (chip ^ mask)] = value
            else:
                x_ref[pl.ds(pl.multiple_of(part * half + (chip ^ mask) * own, own), own), :] = value
    for at in range(2 * half // own if spread else 0):
        x_ref[at * own : (at + 1) * own, :] = spread[0][at]
    rhs_ref[...] = apply_down(x_ref, f0, s0, pairs(down[4:]))
    energy = jnp.full((2 * half, 1), jnp.sum(ea[...] + eb[...]), f32)
    extra = tail(row_squares(rhs_ref[...]), energy)
    front = outs[0].shape[1] - LANES
    project(rhs_ref, f1, s1, pairs(down[:4]), slice(0, front), *outs, bit, extra)


def back_kernel(bit, *refs):
    value_ref, down, outs, scratch = refs[0], refs[1:5], refs[5:7], refs[7:]
    shots = down[0].shape[2]
    project(value_ref, *scratch, pairs(down), slice(shots - outs[0].shape[1], shots), *outs, bit)


def front_kernel(bit, *refs):
    pieces, turned, (x_ref, ends_ref, image_ref), scratch = refs[:2], refs[2:6], refs[6:9], refs[9:]
    collect(pieces, x_ref, bit, ends_ref)
    image_ref[...] = apply_down(x_ref, *scratch, pairs(turned), slice(0, x_ref.shape[1]))


def first_kernel(bits, receivers, *refs):
    pieces, (before_ref, ends_ref, part_ref, rhs_ref, *refs) = refs[:2], refs[2:]
    down, refs = refs[:8], refs[8:]
    (x_ref, scalar_ref, image_ref, residual_ref, *outs), (f0, s0, f1, s1) = refs[:6], refs[6:]
    front = before_ref.shape[1]
    collect(pieces, x_ref, bits[1])
    norm = both(ends_ref[:, 0:1])
    damping = damping_ratio * ends_ref[:, 1:2] / receivers
    image = part_ref[...] + apply_down(x_ref, f0, s0, pairs(down[4:]), slice(front, None)) + damping * rhs_ref[...]
    image_ref[...] = image
    alpha = norm / (both(row_squares(before_ref[...]) + row_squares(x_ref[...])) + damping * norm)
    residual = rhs_ref[...] - alpha * image
    residual_ref[...] = residual
    scalar_ref[...] = tail(norm, damping, alpha)
    project(residual_ref, f1, s1, pairs(down[:4]), slice(0, front), *outs, bits[0], tail(row_squares(residual)))


def last_kernel(bit, side, *refs):
    pieces, (a_ref, ends_ref, part_ref, rhs_ref, before_a, before_b, scalar_ref, image_ref, residual_ref) = refs[:2], refs[2:11]
    turned, (out_ref, x_ref, *scratch) = refs[11:13], refs[13:]
    rows = turned[0].shape[2]
    lines = slice(side * rows, (side + 1) * rows)
    front = a_ref.shape[1]
    collect(pieces, x_ref, bit)
    following = both(ends_ref[:, 0:1])
    norm = scalar_ref[:, 0:1]
    damping = scalar_ref[:, 1:2]
    alpha = scalar_ref[:, 2:3]
    beta = following / norm
    residual = residual_ref[:, lines]
    image = part_ref[:, lines] + apply_down(x_ref, *scratch, pairs(turned), slice(front, None))
    image = image + beta * image_ref[:, lines] + damping * residual
    squares = row_squares(a_ref[...] + beta * before_a[...]) + row_squares(x_ref[...] + beta * before_b[...])
    curvature = both(squares) + damping * (following + beta * following)
    alpha_next = following / curvature
    rhs = rhs_ref[:, lines]
    found = alpha * rhs + alpha_next * (residual + beta * rhs)
    left = residual - alpha_next * image
    out_ref[0] = found
    out_ref[1] = left


def whole_kernel(bit, *refs):
    pieces, (a_ref, ends_ref, part_ref, rhs_ref, before_a, before_b, scalar_ref, image_ref, residual_ref) = refs[:2], refs[2:11]
    turned, (keep_ref, give_ref, x_ref, *scratch) = refs[11:15], refs[15:]
    front = a_ref.shape[1]
    collect(pieces, x_ref, bit)
    following = both(ends_ref[:, 0:1])
    norm = scalar_ref[:, 0:1]
    damping = scalar_ref[:, 1:2]
    alpha = scalar_ref[:, 2:3]
    beta = following / norm
    residual = residual_ref[...]
    image = part_ref[...] + apply_down(x_ref, *scratch, pairs(turned), slice(front, None))
    image = image + beta * image_ref[...] + damping * residual
    squares = row_squares(a_ref[...] + beta * before_a[...]) + row_squares(x_ref[...] + beta * before_b[...])
    curvature = both(squares) + damping * (following + beta * following)
    alpha_next = following / curvature
    rhs = rhs_ref[...]
    found = alpha * rhs + alpha_next * (residual + beta * rhs)
    left = residual - alpha_next * image
    rows = turned[0].shape[2]
    keep_ref[0] = found[:, :rows]
    keep_ref[1] = left[:, :rows]
    give_ref[0] = found[:, rows:]
    give_ref[1] = left[:, rows:]


def order_kernel(own, *refs):
    pieces, (*outs, x_ref) = refs[: 2 * GROUPS], refs[2 * GROUPS :]
    upper = device_bit(0) == 1
    chips = pieces[0].shape[1] // (2 * own)
    for which, out_ref in enumerate(outs):
        for part in range(2):
            for chip in range(chips):
                source = pl.ds((part * chips + chip) * own, own)
                for group in range(GROUPS):
                    mine = pieces[2 * group][which, source, :]
                    other = pieces[2 * group + 1][which, source, :]
                    base = (2 * chip * GROUPS + group) * own
                    x_ref[base : base + own, :] = jnp.where(upper, other, mine)
                    base += GROUPS * own
                    x_ref[base : base + own, :] = jnp.where(upper, mine, other)
            out_ref[part] = x_ref[...].T


class Sum:
    def __init__(self, swap, order, pair):
        self.swap, self.order, self.at = swap, order, 0
        self.keep, give = pair
        self.other = swap(give, order[0])

    def step(self):
        self.at += 1
        self.keep = self.keep + self.other
        self.other = self.swap(self.keep, self.order[self.at % len(self.order)])


def body(down_spectra, up_sources, *, count, receivers):
    chip_bits = list(range(1, count.bit_length() - 1))
    orders = (chip_bits, chip_bits[::-1])
    ends = (chip_bits[0], chip_bits[-1])
    rows, shots = down_spectra.shape[1:]
    own = up_sources.shape[1] // GROUPS
    chips = count // 2
    packed = 2 * chips * own
    front = shots // 2

    def swap(value, bit):
        return lax.ppermute(value, "rcv", [(at, at ^ (1 << bit)) for at in range(count)])

    def jump(value, mask):
        return lax.ppermute(value, "rcv", [(at, at ^ (mask << 1)) for at in range(count)])

    other_down = swap(down_spectra, 0)
    masks = sorted(range(chips), key=lambda mask: mask.bit_count())
    sources = []
    for group in range(GROUPS):
        part = up_sources[:, group * own : (group + 1) * own]
        sources.append([jump(part, mask) if mask else part for mask in masks])
    plain_a, turned_a, energy_a = split(pltpu.with_memory_space_constraint(down_spectra, pltpu.HBM))
    plain_b, turned_b, energy_b = split(other_down)
    turned = (*turned_a, *turned_b)
    down = (*plain_a, *plain_b, *turned)

    wide = [((2 * packed, shots), bf16)] * 2
    narrow = [((2 * packed, front), bf16)] * 2
    short = [((2 * packed, 2 * rows), bf16)] * 2
    lines = ((packed, 2 * rows), f32)
    every = ((packed, shots), f32)
    ranged = ((packed, front), f32)
    small = ((packed, LANES), f32)
    work = 2 * 2 * 2 * (3 * packed) * rows * shots
    sent_0 = [((packed // 2, front + LANES), f32)] * 2
    sent_1 = [((packed // 2, front), f32)] * 2
    spread = [((packed // own, own, shots), f32)] if own % 8 else []
    plain = (*plain_a, *plain_b)

    done = {}

    def after(name, *values):
        for earlier in ORDER.get(name, ()):
            values = lax.optimization_barrier((done[earlier], *values))[1:]
        return values

    def launch(name, kernel, outs, args, scratch, flops):
        first, *rest = args
        results = call(kernel, outs, (*after(name, first), *rest), scratch, int(flops * COST.get(name, 1)))
        done[name] = results[0]
        return results

    def step(name, total):
        (total.keep,) = after(name, total.keep)
        total.step()
        done[name] = total.keep

    def way(name, which):
        return which ^ (name[0] == "b")

    def start(name, which, pair):
        return Sum(swap, orders[way(name, which)], pair)

    def back(name, value):
        kernel = functools.partial(back_kernel, ends[way(name, 1)])
        return start(name, 1, launch(name, kernel, sent_1, (value, *plain), short, work))

    def lead(name, total):
        kernel, pieces = functools.partial(front_kernel, ends[way(name, 0)]), (total.keep, total.other)
        return launch(name, kernel, [ranged, small, lines], (*pieces, *turned), narrow, work)

    def open_group(name, source):
        rhs, *pair = launch(
            name,
            functools.partial(rhs_kernel, ends[way(name, 0)], masks),
            [lines] + sent_0,
            (*source, *down, energy_a, energy_b),
            [every] + wide + short + spread,
            3 * work,
        )
        return rhs, start(name, 0, pair)

    def middle(name, total, led, rhs):
        before, norms, part = led
        x, scalars, image, residual, *pair = launch(
            name,
            functools.partial(first_kernel, (ends[way(name, 0)], ends[way(name, 1)]), receivers),
            [ranged, small, lines, lines] + sent_0,
            (total.keep, total.other, before, norms, part, rhs, *down),
            narrow + short,
            2 * work,
        )
        return (rhs, before, x, scalars, image, residual), start(name, 0, pair)

    def close(name, total, led, kept):
        if name[0] == "a":
            keep, give = launch(
                name,
                functools.partial(whole_kernel, ends[way(name, 1)]),
                [((2, packed, rows), f32)] * 2,
                (total.keep, total.other, *led, *kept, *turned),
                [ranged] + narrow,
                work,
            )
            return keep, swap(give, 0)
        results = []
        for side in (1, 0):
            (piece,) = call(
                functools.partial(last_kernel, ends[way(name, 1)], side),
                [((2, packed, rows), f32)],
                (*after(name, total.keep), total.other, *led, *kept, *turned[2 * side : 2 * side + 2]),
                [ranged] + narrow,
                int(work // 2),
            )
            results.append(piece)
        give, keep = results
        return keep, swap(give, 0)

    def rounds(tag, a0, a1, b0, pending):
        step("a0" + tag, a0)
        step("a1" + tag, a1)
        b1 = back("bC" + tag, pending)
        for turn in range(2, len(chip_bits) + 1):
            end = tag + str(turn)
            step("a0" + end, a0)
            step("b0" + end, b0)
            step("b1" + end, b1)
            step("a1" + end, a1)
        led = lead("aL" + tag, a0)
        step("b0" + tag, b0)
        step("b1" + tag, b1)
        return b1, led

    rhs_a, a0 = open_group("aR", sources[0])
    a1 = back("aC", rhs_a)
    rhs_b, b0 = open_group("bR", sources[1])
    b1, led = rounds("", a0, a1, b0, rhs_b)
    kept_a, a0 = middle("aM", a1, led, rhs_a)
    a1 = back("aC.", kept_a[-1])
    led = lead("bL", b0)
    kept_b, b0 = middle("bM", b1, led, rhs_b)
    b1, led = rounds(".", a0, a1, b0, kept_b[-1])
    results = [close("aE", a1, led, kept_a)]
    led = lead("bL.", b0)
    results.append(close("bE", b1, led, kept_b))

    pieces = [piece for pair in results for piece in pair]
    columns = GROUPS * packed
    return tuple(call(functools.partial(order_kernel, own), [((2, rows, columns), f32)] * 2, pieces, [((columns, rows), f32)]))


def solution(mesh):
    count = mesh.shape["rcv"]

    def run(down_spectra, up_sources):
        return body(down_spectra, up_sources, count=count, receivers=down_spectra.shape[1] * count)

    specs = (P("cuts", "rcv", None), P("cuts", "rcv", None))
    return jax.shard_map(run, mesh=mesh, in_specs=specs, out_specs=specs, check_vma=False)
```
